128 devices in a mesh: grp: 8 (over y, core), fsdp: 16 (over x, z).
Axes of the slice: x: 4, y: 4, z: 4, core: 2. Of those that a mesh axis runs over, the one named last changes fastest.
Arguments:
- tokens: bfloat16 [24576, 8192], P(('grp', 'fsdp')), may hold values from -6 to 6
- targets: bfloat16 [24576, 1024], P(('grp', 'fsdp')), may hold values from -6 to 6
- row_owner_user: int32 [24576, 1], P(('grp', 'fsdp')), may hold values from 0 to 127; in each aligned block of 192 rows (0 to 191, 192 to 383, ...) at most 2 rows name the same one
- device_row_count: int32 [128], P(('grp', 'fsdp')), may hold values from 1 to 192, 18432 in all
- user_row_cap: int32 [128], replicated, may hold values from 48 to 383
- value_weight: bfloat16 [8192, 1024], P('fsdp'), may hold values from -0.0625 to 0.0625
- adapter_down: bfloat16 [8192, 64], replicated, may hold values from -0.0625 to 0.0625
- adapter_up: bfloat16 [64, 1024], replicated, may hold values from -0.75 to 0.75
- clip_norm_bound: float32 [1], replicated, may hold values from 2 to 6
- down_noise: float32 [8192, 64], P(('grp', 'fsdp')), may hold values from -0.12 to 0.12
- up_noise: float32 [64, 1024], P(None, ('grp', 'fsdp')), may hold values from -0.12 to 0.12
Outputs:
- update_a: float32 [8192, 64], P(('grp', 'fsdp'))
- update_b: float32 [64, 1024], P(None, ('grp', 'fsdp'))
The draws below stay inside these ranges and needn't reach their ends.
Inputs may be any that keep to these rules, and one draw needn't show every extreme that they name: `row_owner_user`: within the rows of one device (aligned blocks of 192 rows) no user is named by more than 2 rows, a bound that some block reaches. `device_row_count`: the counts sum to 18432.
All inputs are finite; a program needn't handle non-finite values. No bound on the sum of `device_row_count` on one device may be relied on, other than what follows from the above.
Results may differ from the reference program's by a relative error of at most 0.00084.
Values may be sent and summed in bfloat16 or wider, within the bound.
A program may use at most 128 MiB of HBM per device.

```python
import math
import jax
import jax.numpy as jnp
import numpy as np
from jax import lax

MODEL_WIDTH = 8192
VALUE_WIDTH = 1024
ADAPTER_RANK = 64
STEPS = 2
TOK_DEV = 192
USERS = 128
MOST = 2
SLOTS = 256
TOKENS = 24576
N_GRP = 8
N_FSDP = 16
DEVICES = 128


def with_ends(drawn, own_key, low, high):
    spot = [jax.random.randint(jax.random.fold_in(own_key, axis), (), 0, length) for axis, length in enumerate(drawn.shape)]
    longest = drawn.shape.index(max(drawn.shape))
    neighbour = spot[:longest] + [(spot[longest] + 1) % drawn.shape[longest]] + spot[longest + 1:]
    return drawn.at[tuple(spot)].set(low).at[tuple(neighbour)].set(high)


def levels(rng, dims, pieces, least, largest):
    def one(axis_at, shards_of):
        heights = jax.random.uniform(jax.random.fold_in(jax.random.fold_in(rng, 6), axis_at), (shards_of,), jnp.float32, least / len(pieces), largest / len(pieces))
        return jnp.repeat(jnp.exp(heights), dims[axis_at] // shards_of).reshape((-1,) + (1,) * (len(dims) - axis_at - 1))

    level = one(*pieces[0])
    for cut in pieces[1:]:
        level = level * one(*cut)
    return level


def length_profile(count, total, bound, lean):
    weights = [(1 << 20) // math.isqrt(grade ** lean) + 1 for grade in range(2, count + 1)]
    surplus, holding = total - bound - (count - 1), [1] * (count - 1)
    while surplus > 0:
        free = [i for i in range(count - 1) if holding[i] < bound]
        pool, budget = sum([weights[i] for i in free]), surplus
        for i in free:
            addition = min(bound - holding[i], max(1, budget * weights[i] // pool), surplus)
            holding[i] = holding[i] + addition
            surplus = surplus - addition
    return np.array([bound] + holding)


def ragged(key, number_of, total, reach, lean):
    if number_of == 2:
        one = jax.random.randint(key, (), max(1, total - reach), min(reach, total - 1) + 1)
        return jnp.stack([one, total - one])
    sizes = jnp.asarray(length_profile(number_of, total, reach, lean), jnp.int32)
    pairs = (number_of - 1) // 2
    source_of, sink = sizes[1:1 + 2 * pairs:2], sizes[2:2 + 2 * pairs:2]
    slack = jnp.minimum(source_of - 1, reach - sink)
    passed = jax.random.randint(jax.random.fold_in(key, 1), (pairs,), 0, 1 << 20) % (slack + 1)
    sizes = sizes.at[1:1 + 2 * pairs:2].set(source_of - passed).at[2:2 + 2 * pairs:2].set(sink + passed)
    return sizes[jax.random.permutation(jax.random.fold_in(key, 2), number_of)]


def routed_block(stream_key, own, number, rows, amount, top, limit, skew):
    sequence = jax.random.permutation(stream_key, amount)
    crowded, usual = load_shares(amount, rows * top, limit, skew, True), load_shares(amount, rows * top, limit, skew, False)
    places = jnp.arange(amount)

    def named(lengths, offset_by):
        used = int((lengths > 0).sum())
        fixed = max(1, used // 4)
        shifted = fixed + (places - fixed + offset_by * (used - fixed)) % max(1, amount - fixed)
        return jnp.zeros((amount,), jnp.int32).at[sequence[jnp.where(places < fixed, places, shifted)]].set(jnp.asarray(lengths, jnp.int32))

    lengths = jnp.where(number % 4 == 0, named(crowded, number // 4), named(usual, number - number // 4 - 1))
    mixed = jax.random.permutation(jax.random.fold_in(own, 3), amount)
    giver, sink = mixed[0:amount // 2 * 2:2], mixed[1:amount // 2 * 2:2]
    room = jnp.minimum(lengths[giver] - 1, limit - lengths[sink]) // 2
    room = jnp.where((giver == sequence[0]) | (sink == sequence[0]) | (lengths[sink] == 0), 0, jnp.maximum(room, 0))
    shifted = jax.random.randint(jax.random.fold_in(own, 4), (amount // 2,), 0, 1 << 20) % (room + 1)
    lengths = lengths.at[giver].add(-shifted).at[sink].add(shifted)
    members = jnp.searchsorted(jnp.cumsum(lengths), jnp.arange(rows * top), side="right").astype(jnp.int32)
    table = members.reshape(top, rows).T
    table = table[jax.random.permutation(jax.random.fold_in(own, 1), rows)]
    offset_by = jax.random.randint(jax.random.fold_in(own, 2), (rows, 1), 0, top)
    return jnp.take_along_axis(table, (jnp.arange(top)[None, :] + offset_by) % top, axis=1)


def load_shares(amount, total, limit, skew, full):
    weights = [(1 << 20) // math.isqrt(standing ** skew) + 1 for standing in range(1, amount + 1)]
    largest = limit if full else min(limit, max(-(-total // amount), total * weights[0] // sum(weights)))
    least = 1 if total - largest >= amount - 1 else 0
    given, rest = [largest] + [least] * (amount - 1), total - largest - least * (amount - 1)
    while rest > 0:
        candidates = [i for i in range(1, amount) if given[i] < largest] or [i for i in range(1, amount) if given[i] < limit]
        whole, left = sum([weights[i] for i in candidates]), rest
        for i in candidates:
            addition = min(limit - given[i], max(1, left * weights[i] // whole), rest)
            given[i] = given[i] + addition
            rest = rest - addition
    return np.array(given)


def gaussian(own_key, shape, width, reach, shards=(), held_as=jnp.bfloat16):
    array = width * jax.random.normal(own_key, shape, jnp.float32)
    if shards:
        array = array * levels(own_key, shape, shards, -0.22, 0.18)
    return jnp.clip(array, -reach, reach).astype(held_as)


def setup_inputs(seed: int = 0) -> dict:
    streams_of = jax.random.split(jax.random.key(seed), 12)
    tokens = gaussian(streams_of[0], (TOKENS, MODEL_WIDTH), 1.0, 6.0, ((0, 128),))
    targets = gaussian(streams_of[1], (TOKENS, VALUE_WIDTH), 1.0, 6.0, ((0, 128),))
    row_owner_user_keys = jax.random.split(jax.random.fold_in(streams_of[2], 1), TOKENS // TOK_DEV)
    row_owner_user_turns = jax.random.permutation(jax.random.fold_in(streams_of[2], 3), TOKENS // TOK_DEV)
    row_owner_user = jax.vmap(lambda own, number: routed_block(jax.random.fold_in(streams_of[2], 2), own, number, TOK_DEV, USERS, 1, MOST, 2))(row_owner_user_keys, row_owner_user_turns).reshape((TOKENS, 1))
    device_row_count = ragged(streams_of[3], DEVICES, 3 * TOKENS // 4, TOK_DEV, 2).astype(jnp.int32)
    user_row_cap = with_ends(jax.random.randint(streams_of[4], (USERS,), TOK_DEV // 4, 2 * TOK_DEV), jax.random.fold_in(streams_of[4], 1), TOK_DEV // 4, (2 * TOK_DEV) - 1).astype(jnp.int32)
    value_weight = gaussian(streams_of[5], (MODEL_WIDTH, VALUE_WIDTH), MODEL_WIDTH ** -0.5, 0.0625, ((0, 16),))
    adapter_down = gaussian(streams_of[6], (MODEL_WIDTH, ADAPTER_RANK), MODEL_WIDTH ** -0.5, 0.0625)
    adapter_up = gaussian(streams_of[7], (ADAPTER_RANK, VALUE_WIDTH), ADAPTER_RANK ** -0.5, 0.75)
    clip_norm_bound = jnp.clip(jax.random.uniform(streams_of[8], (1,), jnp.float32, 2.0, 6.0), 2.0, 6.0)
    down_noise = gaussian(streams_of[9], (MODEL_WIDTH, ADAPTER_RANK), 0.02, 0.12, ((0, 128),), jnp.float32)
    up_noise = gaussian(streams_of[10], (ADAPTER_RANK, VALUE_WIDTH), 0.02, 0.12, ((1, 128),), jnp.float32)
    return {"tokens": tokens, "targets": targets, "row_owner_user": row_owner_user, "device_row_count": device_row_count, "user_row_cap": user_row_cap, "value_weight": value_weight, "adapter_down": adapter_down, "adapter_up": adapter_up, "clip_norm_bound": clip_norm_bound, "down_noise": down_noise, "up_noise": up_noise}


adapter_scale = 2.0
learn_rate = 0.05
epsilon = 1e-06

def adapter_step(input_rows, frozen_output, target_value, live_mask, capped_value, adapter_down, adapter_up, clipped_value_rows):
    current_down = adapter_down.astype(jnp.float32)
    current_up = adapter_up.astype(jnp.float32)
    for repeat in range(STEPS):
        a_half = current_down.astype(jnp.bfloat16)
        half_up_matrix = current_up.astype(jnp.bfloat16)
        hidden_input = jnp.dot(input_rows, a_half, preferred_element_type=jnp.float32).astype(jnp.bfloat16)
        value_output = frozen_output + adapter_scale * jnp.dot(hidden_input, half_up_matrix, preferred_element_type=jnp.float32)
        residual_error = (live_mask[:, None] * (value_output - target_value.astype(jnp.float32)) / capped_value).astype(jnp.bfloat16)
        up_gradient = adapter_scale * lax.dot_general(hidden_input, residual_error, (((0,), (0,)), ((), ())), preferred_element_type=jnp.float32)
        backward_pass = jnp.dot(residual_error, half_up_matrix.T, preferred_element_type=jnp.float32).astype(jnp.bfloat16)
        down_gradient = adapter_scale * lax.dot_general(input_rows, backward_pass, (((0,), (0,)), ((), ())), preferred_element_type=jnp.float32)
        current_down = current_down - learn_rate * down_gradient
        current_up = current_up - learn_rate * up_gradient
    down_delta = current_down - adapter_down.astype(jnp.float32)
    up_delta = current_up - adapter_up.astype(jnp.float32)
    total = jnp.sum(down_delta * down_delta) + jnp.sum(up_delta * up_delta)
    factor = jnp.minimum(1.0, clipped_value_rows / jnp.sqrt(total + epsilon))
    return (factor * down_delta, factor * up_delta)

def reference(tokens, targets, row_owner_user, device_row_count, user_row_cap, value_weight, adapter_down, adapter_up, clip_norm_bound, down_noise, up_noise):
    devices = N_GRP * N_FSDP
    user_of = row_owner_user[:, 0].reshape(devices, TOK_DEV)
    position = jnp.arange(TOK_DEV, dtype=jnp.int32)
    valid = position[None, :] < device_row_count[:, None]
    onehot = (user_of[:, :, None] == jnp.arange(USERS, dtype=jnp.int32)[None, None, :]).astype(jnp.int32)
    before_all = jnp.cumsum(onehot, axis=1) - onehot
    row_rank = lax.optimization_barrier(jnp.sum(before_all * onehot, axis=2))
    valid_hot = onehot * valid[:, :, None].astype(jnp.int32)
    flat = valid_hot.reshape(devices * TOK_DEV, USERS)
    before_valid = (jnp.cumsum(flat, axis=0) - flat).reshape(devices, TOK_DEV, USERS)
    earlier = lax.optimization_barrier(jnp.sum(before_valid * onehot, axis=2))
    cap_row = user_row_cap[user_of]
    kept = valid & (earlier < cap_row)
    source = jnp.arange(devices, dtype=jnp.int32)[:, None]
    slot_key = user_of * SLOTS + source * MOST + row_rank
    slot_key = jnp.where(kept, slot_key, USERS * SLOTS).reshape(-1).astype(jnp.int32)
    row_index = jnp.arange(TOKENS, dtype=jnp.int32)
    table = jnp.full((USERS * SLOTS,), TOKENS, dtype=jnp.int32).at[slot_key].set(row_index, mode='drop')
    table = table.reshape(USERS, SLOTS)
    tokens_pad = jnp.concatenate([tokens, jnp.zeros((1, MODEL_WIDTH), tokens.dtype)], axis=0)
    targets_pad = jnp.concatenate([targets, jnp.zeros((1, VALUE_WIDTH), targets.dtype)], axis=0)
    clipped_value_rows = clip_norm_bound[0]

    def one_user(carry, inputs):
        indices, capped_value = inputs
        input_rows = tokens_pad[indices]
        target_value = targets_pad[indices]
        live_mask = (indices < TOKENS).astype(jnp.float32)
        frozen_output = jnp.dot(input_rows, value_weight, preferred_element_type=jnp.float32)
        down_partial, up_partial = adapter_step(input_rows, frozen_output, target_value, live_mask, capped_value.astype(jnp.float32), adapter_down, adapter_up, clipped_value_rows)
        return ((carry[0] + down_partial, carry[1] + up_partial), None)
    start = (jnp.zeros((MODEL_WIDTH, ADAPTER_RANK), jnp.float32), jnp.zeros((ADAPTER_RANK, VALUE_WIDTH), jnp.float32))
    sums, unused = lax.scan(one_user, start, (table, user_row_cap))
    update_a = sums[0] + clipped_value_rows * down_noise
    update_b = sums[1] + clipped_value_rows * up_noise
    return (update_a, update_b)
```

```python
import jax
import jax.numpy as jnp
from jax import lax
from jax.sharding import PartitionSpec as P

STEPS = 2
BOTH = ("grp", "fsdp")
adapter_scale = 2.0
learn_rate = 0.05
epsilon = 1e-06
F32 = jnp.float32
BF16 = jnp.bfloat16


def adapter_step(rows, frozen, goal, live, cap, down, up, bound):
    cur_a, cur_b = down.astype(F32), up.astype(F32)
    for _ in range(STEPS):
        a16, b16 = cur_a.astype(BF16), cur_b.astype(BF16)
        h = jnp.dot(rows, a16, preferred_element_type=F32).astype(BF16)
        y = frozen + adapter_scale * jnp.dot(h, b16, preferred_element_type=F32)
        r = (live[:, None] * (y - goal.astype(F32)) / cap).astype(BF16)
        grad_b = adapter_scale * lax.dot_general(
            h, r, (((0,), (0,)), ((), ())), preferred_element_type=F32
        )
        back = jnp.dot(r, b16.T, preferred_element_type=F32).astype(BF16)
        grad_a = adapter_scale * lax.dot_general(
            rows, back, (((0,), (0,)), ((), ())), preferred_element_type=F32
        )
        cur_a = cur_a - learn_rate * grad_a
        cur_b = cur_b - learn_rate * grad_b
    delta_a = cur_a - down.astype(F32)
    delta_b = cur_b - up.astype(F32)
    total = jnp.sum(delta_a * delta_a) + jnp.sum(delta_b * delta_b)
    factor = jnp.minimum(1.0, bound / jnp.sqrt(total + epsilon))
    return factor * delta_a, factor * delta_b


def body(
    tokens,
    targets,
    row_owner_user,
    device_row_count,
    user_row_cap,
    value_weight,
    adapter_down,
    adapter_up,
    clip_norm_bound,
    down_noise,
    up_noise,
):
    devices = lax.axis_size(BOTH)
    myself = lax.axis_index(BOTH)
    groups = lax.axis_size("grp")
    core = lax.axis_index("grp") % 2
    per_dev, width = tokens.shape
    kv_width = targets.shape[1]
    users = user_row_cap.shape[0]
    most = 3 * per_dev // (2 * devices)
    slots = devices * most
    half = kv_width // 2

    w_half = lax.dynamic_slice(
        value_weight, (0, core * half), (value_weight.shape[0], half)
    )
    w_mine = lax.all_gather(w_half, "fsdp", axis=0, tiled=True)

    user_of = row_owner_user[:, 0]
    position = jnp.arange(per_dev, dtype=jnp.int32)
    same = (user_of[:, None] == user_of[None, :]) & (position[None, :] < position[:, None])
    rank = jnp.sum(same.astype(jnp.int32), axis=1)
    slot = user_of * most + rank
    place = (jnp.arange(slots, dtype=jnp.int32)[:, None] == slot[None, :]).astype(BF16)
    in_use = (position < device_row_count[0]).astype(BF16)
    flags = jnp.broadcast_to(in_use[:, None], (per_dev, 128))

    send = jnp.concatenate(
        [
            jnp.dot(place, tokens, preferred_element_type=F32).astype(BF16),
            jnp.dot(place, targets, preferred_element_type=F32).astype(BF16),
            jnp.dot(place, flags, preferred_element_type=F32).astype(BF16),
        ],
        axis=1,
    )
    got = lax.all_to_all(
        send.reshape(devices, most, -1), BOTH, split_axis=0, concat_axis=0, tiled=True
    ).reshape(slots, -1)
    rows = got[:, :width]
    goal = got[:, width : width + kv_width]
    used = got[:, width + kv_width].astype(F32)
    order = jnp.arange(slots, dtype=jnp.int32)
    before = (order[None, :] < order[:, None]).astype(F32)
    earlier = jnp.sum(before * used[None, :], axis=1)
    cap = jnp.sum(
        jnp.where(jnp.arange(users, dtype=jnp.int32) == myself, user_row_cap, 0)
    ).astype(F32)
    live = jnp.where((used > 0.5) & (earlier < cap), 1.0, 0.0).astype(F32)

    pairs = [(i, i ^ 1) for i in range(groups)]
    w_mine, rows = lax.optimization_barrier((w_mine, rows))
    w_other = lax.ppermute(w_mine, "grp", pairs)
    f_mine = jnp.dot(rows, w_mine, preferred_element_type=F32)
    f_other = jnp.dot(rows, w_other, preferred_element_type=F32)
    frozen = jnp.concatenate(
        [jnp.where(core == 0, f_mine, f_other), jnp.where(core == 0, f_other, f_mine)],
        axis=1,
    )
    bound = clip_norm_bound[0]
    part_a, part_b = adapter_step(
        rows, frozen, goal, live, cap, adapter_down, adapter_up, bound
    )
    a_rows, rank_dim = part_a.shape[0] // devices, part_a.shape[1]
    b_cols = part_b.shape[1] // devices
    out = jnp.concatenate(
        [
            part_a.reshape(devices, a_rows * rank_dim),
            part_b.reshape(rank_dim, devices, b_cols)
            .transpose(1, 0, 2)
            .reshape(devices, rank_dim * b_cols),
        ],
        axis=1,
    ).reshape(devices, -1, 128)
    summed = jnp.sum(
        lax.all_to_all(out, BOTH, split_axis=0, concat_axis=0, tiled=True), axis=0
    ).reshape(-1)
    cut = a_rows * rank_dim
    update_a = summed[:cut].reshape(a_rows, rank_dim) + bound * down_noise
    update_b = summed[cut:].reshape(rank_dim, b_cols) + bound * up_noise
    return update_a, update_b


def solution(mesh):
    in_specs = (
        P(BOTH, None),
        P(BOTH, None),
        P(BOTH, None),
        P(BOTH),
        P(),
        P("fsdp", None),
        P(),
        P(),
        P(),
        P(BOTH, None),
        P(None, BOTH),
    )
    out_specs = (P(BOTH, None), P(None, BOTH))
    return jax.shard_map(
        body, mesh=mesh, in_specs=in_specs, out_specs=out_specs, check_vma=False
    )
```

```python
import functools

import jax
import jax.numpy as jnp
from jax import lax
from jax.experimental import pallas as pl
from jax.experimental.pallas import tpu as pltpu
from jax.sharding import PartitionSpec as P

STEPS = 2
BOTH = ("grp", "fsdp")
MESH = pl.DeviceIdType.MESH
scale = 2.0
rate = 0.05
epsilon = 1e-06
F32 = jnp.float32
BF16 = jnp.bfloat16
SIDE = 4
ROWS_A = 64
SLAB = 72


def mm(a, b, ca, cb):
    return lax.dot_general(a, b, (((ca,), (cb,)), ((), ())), preferred_element_type=F32)


def slab_place(p):
    y, c, x, zh = p // 16, p // 8 % 2, p // 2 % 4, p % 2
    def code(i):
        u, v = i // 2, (i ^ (i // 2)) & 1
        return (v, u) if c == 0 else (u, v)
    return (c, *code(y), *code(x), zh)


def adapter_kernel(
    width, kv, chunk, f_ref, i_ref, got_ref, wm_ref, wo_ref, at_ref, b_ref, out_ref, mine, other, hid, a1, bcur, acc
):
    step = pl.program_id(0)
    steps = width // chunk
    slots = got_ref.shape[0]

    @pl.when(step == 0)
    def _():
        mine[...] = jnp.zeros_like(mine)
        other[...] = jnp.zeros_like(other)
        hid[...] = jnp.zeros_like(hid)

    def part(k):
        return pl.ds(pl.multiple_of(k * chunk, chunk), chunk)

    rows = got_ref[:, part(step)]
    mine[...] += mm(rows, wm_ref[...], 1, 0)
    other[...] += mm(rows, wo_ref[...], 1, 0)
    hid[...] += mm(rows, at_ref[:, part(step)], 1, 1)

    @pl.when(step == steps - 1)
    def _():
        cap, bound, core = f_ref[0], f_ref[1], i_ref[0]
        used = got_ref[:, width + kv :]
        r_i = lax.broadcasted_iota(jnp.int32, (slots, slots), 0)
        c_i = lax.broadcasted_iota(jnp.int32, (slots, slots), 1)
        before = jnp.where(c_i < r_i, 1.0, 0.0).astype(BF16)
        earlier = mm(before, used, 1, 0)
        live = jnp.where((used.astype(F32) > 0.5) & (earlier < cap), 1.0 / cap, 0.0)
        live = jnp.concatenate([live] * (kv // live.shape[1]), axis=1)
        first, second = mine[...], other[...]
        base = jnp.concatenate(
            [jnp.where(core == 0, first, second), jnp.where(core == 0, second, first)], axis=1
        ) - got_ref[:, width : width + kv].astype(F32)

        def errors(h, b16):
            y = base + scale * mm(h, b16, 1, 0)
            r = (live * y).astype(BF16)
            return r, mm(r, b16, 1, 1).astype(BF16), scale * mm(h, r, 0, 0)

        b0 = b_ref[...]
        h1 = hid[...].astype(BF16)
        _, back, grad_b = errors(h1, b0)
        bcur[...] = b0.astype(F32) - rate * grad_b
        hid[...] = jnp.zeros_like(hid)

        @pl.loop(0, steps)
        def _(k):
            x = got_ref[:, part(k)]
            a = at_ref[:, part(k)].astype(F32) - rate * (scale * mm(back, x, 0, 0))
            a1[:, part(k)] = a
            hid[...] += mm(x, a.astype(BF16), 1, 1)

        h2 = hid[...].astype(BF16)
        _, back2, grad_b2 = errors(h2, bcur[...].astype(BF16))
        delta_b = (bcur[...] - rate * grad_b2) - b0.astype(F32)
        acc[...] = jnp.zeros_like(acc)

        @pl.loop(0, steps)
        def _(k):
            x = got_ref[:, part(k)]
            d = (a1[:, part(k)] - rate * (scale * mm(back2, x, 0, 0))) - at_ref[:, part(k)].astype(F32)
            a1[:, part(k)] = d
            acc[...] += jnp.sum((d * d).reshape(d.shape[0], chunk // 128, 128), axis=1)

        total = jnp.sum(acc[...]) + jnp.sum(delta_b * delta_b)
        factor = jnp.minimum(1.0, bound / jnp.sqrt(jnp.broadcast_to(total, (8, 128)) + epsilon))
        fa = jnp.concatenate([factor] * (ROWS_A // 8), axis=0)
        pairs = width // 128
        bt = (delta_b * factor[:1, :1]).T.reshape(pairs, 16, ROWS_A)
        packed = jnp.concatenate([bt[:, :8, :], bt[:, 8:, :]], axis=2)
        for p in range(pairs):
            place = slab_place(p)
            out_ref[(*place, slice(0, ROWS_A), slice(None))] = fa * a1[:, p * 128 : (p + 1) * 128]
            out_ref[(*place, slice(ROWS_A, SLAB), slice(None))] = packed[p]


def adapter(got, w_mine, w_other, at, b, floats, ints, width, kv):
    slots, cols = got.shape
    chunk = 1024
    return pl.pallas_call(
        functools.partial(adapter_kernel, width, kv, chunk),
        grid=(width // chunk,),
        out_shape=jax.ShapeDtypeStruct((2, 2, 2, 2, 2, 2, SLAB, 128), F32),
        in_specs=[
            pl.BlockSpec(memory_space=pltpu.SMEM),
            pl.BlockSpec(memory_space=pltpu.SMEM),
            pl.BlockSpec((slots, cols), lambda k: (0, 0), pipeline_mode=pl.Buffered(1)),
            pl.BlockSpec((chunk, kv // 2), lambda k: (k, 0)),
            pl.BlockSpec((chunk, kv // 2), lambda k: (k, 0)),
            pl.BlockSpec(at.shape, lambda k: (0, 0), pipeline_mode=pl.Buffered(1)),
            pl.BlockSpec(b.shape, lambda k: (0, 0), pipeline_mode=pl.Buffered(1)),
        ],
        out_specs=pl.BlockSpec(
            (2, 2, 2, 2, 2, 2, SLAB, 128), lambda k: (0,) * 8, pipeline_mode=pl.Buffered(1)
        ),
        scratch_shapes=[
            pltpu.VMEM((slots, kv // 2), F32),
            pltpu.VMEM((slots, kv // 2), F32),
            pltpu.VMEM((slots, at.shape[0]), F32),
            pltpu.VMEM(at.shape, F32),
            pltpu.VMEM(b.shape, F32),
            pltpu.VMEM((at.shape[0], 128), F32),
        ],
        compiler_params=pltpu.CompilerParams(vmem_limit_bytes=40 << 20),
        name="adapter",
    )(floats, ints, got, w_mine, w_other, at, b)


def places():
    g, f = lax.axis_index("grp"), lax.axis_index("fsdp")
    return g // 2, g % 2, f // SIDE, f % SIDE


def low(i):
    return i + 1 - 2 * (i % 2)


def mirror(i):
    return 3 - i


def bits(i, c):
    u = i // 2
    v = (i + i // 2) % 2
    return c * u + (1 - c) * v, c * v + (1 - c) * u


def sides(i, c):
    return c * mirror(i) + (1 - c) * low(i), c * low(i) + (1 - c) * mirror(i)


CUT = 40


def reduce_kernel(
    s_ref, out_ref, a0, a1, a2, a3, a4, a5, a6, s1, b0, b1, b2, b3, b4, b5, b6, t1, send, recv
):
    y, c, x, z = places()

    def dev(y=y, c=c, x=x, z=z):
        return (y * 2 + c, x * SIDE + z)

    yb, xb, zh = bits(y, c), bits(x, c), z // 2
    yn, xn = sides(y, c), sides(x, c)
    across = dev(c=1 - c)
    over_y = [dev(y=n) for n in yn]
    over_x = [dev(x=n) for n in xn]
    over_z = [dev(z=mirror(z)), dev(z=low(z))]
    partners = [across, *over_y, *over_x, *over_z]
    barrier = pltpu.get_barrier_semaphore()
    for d in partners:
        pl.semaphore_signal(barrier, inc=1, device_id=d, device_id_type=MESH)
    pl.semaphore_wait(barrier, len(partners))

    started = []

    def go(src, dst, to):
        n = len(started)
        d = pltpu.make_async_remote_copy(
            src_ref=src, dst_ref=dst, send_sem=send.at[n], recv_sem=recv.at[n],
            device_id=to, device_id_type=MESH,
        )
        d.start()
        started.append(d)
        return d

    top, low_rows = slice(0, CUT), slice(CUT, SLAB)
    da = go(s_ref.at[1 - c, :, :, :, :, :, top], a0, across)
    db = go(s_ref.at[1 - c, :, :, :, :, :, low_rows], b0, across)

    da.wait_recv()
    s1[...] = s_ref[c, :, :, :, :, :, top] + a0[...]
    da = go(s1.at[1 - yb[0]], a1, over_y[0])
    db.wait_recv()
    t1[...] = s_ref[c, :, :, :, :, :, low_rows] + b0[...]
    db = go(t1.at[:, :, 1 - xb[0]], b1, over_x[0])

    da.wait_recv()
    a1[...] += s1[yb[0]]
    da = go(a1.at[1 - yb[1]], a2, over_y[1])
    db.wait_recv()
    b1[...] += t1[:, :, xb[0]]
    db = go(b1.at[:, :, 1 - xb[1]], b2, over_x[1])

    da.wait_recv()
    a2[...] += a1[yb[1]]
    da = go(a2.at[1 - xb[0]], a3, over_x[0])
    db.wait_recv()
    b2[...] += b1[:, :, xb[1]]
    db = go(b2.at[1 - yb[0]], b3, over_y[0])

    da.wait_recv()
    a3[...] += a2[xb[0]]
    da = go(a3.at[1 - xb[1]], a4, over_x[1])
    db.wait_recv()
    b3[...] += b2[yb[0]]
    db = go(b3.at[1 - yb[1]], b4, over_y[1])

    da.wait_recv()
    a4[...] += a3[xb[1]]
    da = go(a4.at[1 - zh], a5, over_z[0])
    db.wait_recv()
    b4[...] += b3[yb[1]]
    db = go(b4.at[1 - zh], b5, over_z[0])

    da.wait_recv()
    a5[...] += a4[zh]
    da = go(a5, a6, over_z[1])
    db.wait_recv()
    b5[...] += b4[zh]
    db = go(b5, b6, over_z[1])

    da.wait_recv()
    out_ref[top] = a5[...] + a6[...]
    db.wait_recv()
    out_ref[low_rows] = b5[...] + b6[...]
    for d in started:
        d.wait_send()


def reduce(slabs):
    def halves(n):
        two = (2, 2, 2, 2, 2)
        bufs = [pltpu.VMEM((*two[k:], n, 128), F32) for k in (0, 1, 2, 3, 4, 5)]
        return [bufs[0], *bufs[1:], pltpu.VMEM((n, 128), F32), pltpu.VMEM((*two, n, 128), F32)]

    return pl.pallas_call(
        reduce_kernel,
        out_shape=jax.ShapeDtypeStruct((SLAB, 128), F32),
        in_specs=[pl.BlockSpec(memory_space=pltpu.VMEM)],
        out_specs=pl.BlockSpec(memory_space=pltpu.VMEM),
        scratch_shapes=[
            *halves(CUT),
            *halves(SLAB - CUT),
            pltpu.SemaphoreType.DMA((14,)),
            pltpu.SemaphoreType.DMA((14,)),
        ],
        compiler_params=pltpu.CompilerParams(collective_id=0, has_side_effects=True),
        name="reduce_slabs",
    )(slabs)


def body(
    tokens,
    targets,
    row_owner_user,
    device_row_count,
    user_row_cap,
    value_weight,
    adapter_down,
    adapter_up,
    clip_norm_bound,
    down_noise,
    up_noise,
):
    devices = lax.axis_size(BOTH)
    myself = lax.axis_index(BOTH)
    groups = lax.axis_size("grp")
    core = lax.axis_index("grp") % 2
    per_dev, width = tokens.shape
    kv = targets.shape[1]
    users = user_row_cap.shape[0]
    most = 3 * per_dev // (2 * devices)
    slots = devices * most
    half = kv // 2

    w_half = lax.dynamic_slice(value_weight, (0, core * half), (value_weight.shape[0], half))
    w_mine = lax.all_gather(w_half, "fsdp", axis=0, tiled=True)

    user_of = row_owner_user[:, 0]
    position = jnp.arange(per_dev, dtype=jnp.int32)
    same = (user_of[:, None] == user_of[None, :]) & (position[None, :] < position[:, None])
    rank = jnp.sum(same.astype(jnp.int32), axis=1)
    slot = user_of * most + rank
    place = (jnp.arange(slots, dtype=jnp.int32)[:, None] == slot[None, :]).astype(BF16)
    in_use = (position < device_row_count[0]).astype(BF16)
    flags = jnp.broadcast_to(in_use[:, None], (per_dev, 128))
    cap = jnp.sum(jnp.where(jnp.arange(users, dtype=jnp.int32) == myself, user_row_cap, 0))
    bound = clip_norm_bound[0]
    floats = jnp.stack([cap.astype(F32), bound])
    ints = core.reshape(1)
    at = adapter_down.T

    send = jnp.concatenate(
        [
            jnp.dot(place, tokens, preferred_element_type=F32).astype(BF16),
            jnp.dot(place, targets, preferred_element_type=F32).astype(BF16),
            jnp.dot(place, flags, preferred_element_type=F32).astype(BF16),
        ],
        axis=1,
    )
    got = lax.all_to_all(
        send.reshape(devices, most, -1), BOTH, split_axis=0, concat_axis=0, tiled=True
    ).reshape(slots, -1)

    pairs = [(i, i ^ 1) for i in range(groups)]
    w_mine, got = lax.optimization_barrier((w_mine, got))
    w_other = lax.ppermute(w_mine, "grp", pairs)
    slabs = adapter(got, w_mine, w_other, at, adapter_up, floats, ints, width, kv)
    slab = reduce(slabs)
    odd = myself % 2
    mine = jnp.where(odd == 0, slab[:, :64], slab[:, 64:])
    update_a = mine[:ROWS_A].T + bound * down_noise
    update_b = mine[ROWS_A:].T + bound * up_noise
    return update_a, update_b


def solution(mesh):
    in_specs = (
        P(BOTH, None),
        P(BOTH, None),
        P(BOTH, None),
        P(BOTH),
        P(),
        P("fsdp", None),
        P(),
        P(),
        P(),
        P(BOTH, None),
        P(None, BOTH),
    )
    out_specs = (P(BOTH, None), P(None, BOTH))
    return jax.shard_map(
        body, mesh=mesh, in_specs=in_specs, out_specs=out_specs, check_vma=False
    )
```

```python
import functools

import jax
import jax.numpy as jnp
from jax import lax
from jax.experimental import pallas as pl
from jax.experimental.pallas import tpu as pltpu
from jax.sharding import PartitionSpec as P

STEPS = 2
BOTH = ("grp", "fsdp")
MESH = pl.DeviceIdType.MESH
scale = 2.0
rate = 0.05
epsilon = 1e-06
F32 = jnp.float32
BF16 = jnp.bfloat16
SIDE = 4
ROWS_A = 64
SLAB = 72


def mm(a, b, ca, cb):
    return lax.dot_general(a, b, (((ca,), (cb,)), ((), ())), preferred_element_type=F32)


def slab_place(p):
    y, c, x, zh = p // 16, p // 8 % 2, p // 2 % 4, p % 2
    def code(i):
        u, v = i // 2, (i ^ (i // 2)) & 1
        return (v, u) if c == 0 else (u, v)
    return (c, *code(y), *code(x), zh)


def places():
    g, f = lax.axis_index("grp"), lax.axis_index("fsdp")
    return g // 2, g % 2, f // SIDE, f % SIDE


def low(i):
    return i + 1 - 2 * (i % 2)


def mirror(i):
    return 3 - i


def bits(i, c):
    u = i // 2
    v = (i + i // 2) % 2
    return c * u + (1 - c) * v, c * v + (1 - c) * u


def sides(i, c):
    return c * mirror(i) + (1 - c) * low(i), c * low(i) + (1 - c) * mirror(i)


ROWS_F = 16
ROWS_G = 32
AHEAD = 2
PARTS = 2
PIECE = 256
ORDER = [(1, 0), (0, 1), (3, 0), (0, 3), (1, 1), (3, 3), (1, 3), (3, 1), (2, 0), (0, 2), (2, 1), (1, 2), (2, 3), (3, 2), (2, 2)]


def flip(i, by_low, by_mirror):
    i = i + by_low * (1 - 2 * (i % 2))
    return i + by_mirror * (3 - 2 * i)


def piece(i, h, a, b):
    i0, i1, i2, i3 = i % 2, i // 2 % 2, i // 4 % 2, i // 8
    if h == 1:
        i0, i1, i2, i3 = i1, i0, i3, i2
    return flip(a, i0, i1), flip(b, i2, i3)


def main_kernel(
    f_ref, place_ref, tok_ref, tgt_ref, w_ref, at_ref, b_ref, out_ref,
    st, sx, rt, rx, pt, px, gt, gx, wf, acc, hid, a1, bcur, sq,
    fsend, frecv, gsend, grecv, wsend, wrecv, csend, crecv, local,
):
    y, c, x, z = places()
    g, f = y * 2 + c, x * SIDE + z
    a, b = (1 - c) * x + c * z, (1 - c) * z + c * x
    width = tok_ref.shape[1]
    kv = b_ref.shape[1]
    chunk = sx.shape[2]
    steps = width // chunk
    slots = place_ref.shape[0]
    half = kv // 2

    def column(pos, core):
        return pos[0] * (SIDE - 3 * core) + pos[1] * (1 + 3 * core)

    f_peers = []
    for dx, dz in ORDER:
        f_peers.append((x + dx) % SIDE * SIDE + (z + dz) % SIDE)
    g_peers = []
    for dy, dc in [(1, 0), (3, 1), (3, 0), (1, 1), (2, 0), (2, 1), (0, 1)]:
        g_peers.append((y + dy) % SIDE * 2 + (c + dc) % 2)

    barrier = pltpu.get_barrier_semaphore()
    for to in f_peers:
        pl.semaphore_signal(barrier, inc=1, device_id=(g, to), device_id_type=MESH)
    for to in g_peers:
        pl.semaphore_signal(barrier, inc=1, device_id=(to, f), device_id_type=MESH)

    keep = []
    for h in range(PARTS):
        rows = slice(h * PIECE, (h + 1) * PIECE)
        for n in range(2):
            keep.append(
                pltpu.make_async_copy(w_ref.at[rows, n * half : (n + 1) * half], wf.at[n, f, rows], local.at[2 * h + n])
            )
            keep[-1].start()

    place = place_ref[...]
    n_i = lax.broadcasted_iota(jnp.int32, (slots, slots), 0)
    o_i = lax.broadcasted_iota(jnp.int32, (slots, slots), 1)
    old = ((n_i >> 1) & 15) * 16 + (n_i >> 5) * 2 + (n_i & 1)
    turn = jnp.where(o_i == old, 1.0, 0.0).astype(BF16)

    def bufs(k):
        if k == 0:
            return st, rt, pt, gt
        return sx.at[k - 1], rx.at[k - 1], px.at[k - 1], gx.at[k - 1]

    def rows_f(i):
        return pl.ds(pl.multiple_of(i * ROWS_F, ROWS_F), ROWS_F)

    def rows_g(i):
        return pl.ds(pl.multiple_of(i * ROWS_G, ROWS_G), ROWS_G)

    def place_rows(k):
        s = bufs(k)[0]
        source = tgt_ref[...] if k == 0 else tok_ref[:, (k - 1) * chunk : k * chunk]
        s[...] = mm(place, source, 1, 0).astype(BF16)

    def start_f(k):
        s, r, _, _ = bufs(k)
        for to in f_peers:
            pltpu.make_async_remote_copy(
                src_ref=s.at[rows_f(to)], dst_ref=r.at[rows_f(f)], send_sem=fsend.at[k], recv_sem=frecv.at[k],
                device_id=(g, to), device_id_type=MESH,
            ).start()
        r[rows_f(f), :] = s[rows_f(f), :]

    def turn_rows(k):
        _, r, p, q = bufs(k)
        most = r.at[: slots - ROWS_F]
        pltpu.make_async_copy(most, most, frecv.at[k]).wait()
        p[...] = mm(turn, r[...], 1, 0).astype(BF16)
        for to in g_peers:
            pltpu.make_async_remote_copy(
                src_ref=p.at[rows_g(to)], dst_ref=q.at[rows_g(g)], send_sem=gsend.at[k], recv_sem=grecv.at[k],
                device_id=(to, f), device_id_type=MESH,
            ).start()
        q[rows_g(g), :] = p[rows_g(g), :]

    def end_g(k):
        q = bufs(k)[3]
        most = q.at[: slots - ROWS_G]
        pltpu.make_async_copy(most, most, grecv.at[k]).wait()

    def weight(i, h):
        return wf.at[c, column(piece(i, h, a, b), c), h * PIECE : (h + 1) * PIECE]

    def pass_on(i, h):
        level = i.bit_length()
        to_ref = weight(i, h)
        if i == 0:
            src = w_ref.at[h * PIECE : (h + 1) * PIECE, pl.ds(pl.multiple_of(c * half, half), half)]
        else:
            src = to_ref
            pltpu.make_async_copy(src, src, wrecv.at[h, i]).wait()
            swap(i, h)
        for n in range(level, 4):
            to = column(piece(1 << n, h, a, b), c)
            pltpu.make_async_remote_copy(
                src_ref=src, dst_ref=to_ref, send_sem=wsend.at[h], recv_sem=wrecv.at[h, (1 << n) + i],
                device_id=(g, to), device_id_type=MESH,
            ).start()

    def swap(i, h):
        ref = weight(i, h)
        pltpu.make_async_remote_copy(
            src_ref=ref, dst_ref=ref, send_sem=csend.at[h], recv_sem=crecv.at[h, i],
            device_id=(y * 2 + 1 - c, f), device_id_type=MESH,
        ).start()

    def other_column(i, h):
        return column(piece(i, h, b, a), 1 - c)

    def add(n, col, h):
        per = chunk // (PARTS * PIECE)
        x_cols = gx[col // per, :, pl.ds(pl.multiple_of(col % per * (PARTS * PIECE) + h * PIECE, PIECE), PIECE)]
        acc[n] += mm(x_cols, wf[n, col, h * PIECE : (h + 1) * PIECE, :], 1, 0)

    place_rows(0)
    pl.semaphore_wait(barrier, len(f_peers) + len(g_peers))
    for h in range(PARTS):
        pass_on(0, h)
    start_f(0)
    acc[...] = jnp.zeros_like(acc)
    hid[...] = jnp.zeros_like(hid)
    todo = {3: [1], 5: [2, 3], 7: [4, 5, 6, 7]}
    for k in range(1, steps + 1 + AHEAD):
        if k <= steps:
            place_rows(k)
            start_f(k)
        if k >= AHEAD:
            turn_rows(k - AHEAD)
        for i in todo.get(k, []):
            for h in range(PARTS):
                pass_on(i, h)

    end_g(0)
    for k in range(1, steps + 1):
        end_g(k)
        hid[...] += mm(gx[k - 1], at_ref[:, (k - 1) * chunk : k * chunk], 1, 1)
    for d in keep:
        d.wait()
    for n in range(2):
        for h in range(PARTS):
            add(n, f, h)

    @pl.loop(1, 8)
    def _(i):
        for h in range(PARTS):
            add(c, column(piece(i, h, a, b), c), h)
            col = other_column(i, h)
            ref = wf.at[1 - c, col, h * PIECE : (h + 1) * PIECE]
            pltpu.make_async_copy(ref, ref, crecv.at[h, i]).wait()
            add(1 - c, col, h)

    @pl.loop(8, 16)
    def _(i):
        for h in range(PARTS):
            ref = weight(i, h)
            pltpu.make_async_copy(ref, ref, wrecv.at[h, i]).wait()
            swap(i, h)
            add(c, column(piece(i, h, a, b), c), h)

    @pl.loop(8, 16)
    def _(i):
        for h in range(PARTS):
            col = other_column(i, h)
            ref = wf.at[1 - c, col, h * PIECE : (h + 1) * PIECE]
            pltpu.make_async_copy(ref, ref, crecv.at[h, i]).wait()
            add(1 - c, col, h)

    cap, bound = f_ref[0], f_ref[1]
    used = gt[:, kv:]
    before = jnp.where(o_i < n_i, 1.0, 0.0).astype(BF16)
    earlier = mm(before, used, 1, 0)
    live = jnp.where((used.astype(F32) > 0.5) & (earlier < cap), 1.0 / cap, 0.0)
    live = jnp.concatenate([live] * (kv // live.shape[1]), axis=1)
    base = jnp.concatenate([acc[0], acc[1]], axis=1) - gt[:, :kv].astype(F32)

    def part(k):
        return pl.ds(pl.multiple_of(k * chunk, chunk), chunk)

    def errors(h, b16):
        r = (live * (base + scale * mm(h, b16, 1, 0))).astype(BF16)
        return mm(r, b16, 1, 1).astype(BF16), scale * mm(h, r, 0, 0)

    b0 = b_ref[...]
    back, grad_b = errors(hid[...].astype(BF16), b0)
    bcur[...] = b0.astype(F32) - rate * grad_b
    hid[...] = jnp.zeros_like(hid)

    @pl.loop(0, steps)
    def _(k):
        rows = gx[k]
        now = at_ref[:, part(k)].astype(F32) - rate * (scale * mm(back, rows, 0, 0))
        a1[:, part(k)] = now
        hid[...] += mm(rows, now.astype(BF16), 1, 1)

    back2, grad_b2 = errors(hid[...].astype(BF16), bcur[...].astype(BF16))
    delta_b = (bcur[...] - rate * grad_b2) - b0.astype(F32)
    sq[...] = jnp.zeros_like(sq)

    @pl.loop(0, steps)
    def _(k):
        d = (a1[:, part(k)] - rate * (scale * mm(back2, gx[k], 0, 0))) - at_ref[:, part(k)].astype(F32)
        a1[:, part(k)] = d
        sq[...] += jnp.sum((d * d).reshape(d.shape[0], chunk // 128, 128), axis=1)

    total = jnp.sum(sq[...]) + jnp.sum(delta_b * delta_b)
    factor = jnp.minimum(1.0, bound / jnp.sqrt(jnp.broadcast_to(total, (8, 128)) + epsilon))
    fa = jnp.concatenate([factor] * (ROWS_A // 8), axis=0)
    pairs = width // 128
    bt = (delta_b * factor[:1, :1]).T.reshape(pairs, 16, ROWS_A)
    packed = jnp.concatenate([bt[:, :8, :], bt[:, 8:, :]], axis=2)
    for p in range(pairs):
        spot = slab_place(p)
        out_ref[(*spot, slice(0, ROWS_A), slice(None))] = fa * a1[:, p * 128 : (p + 1) * 128]
        out_ref[(*spot, slice(ROWS_A, SLAB), slice(None))] = packed[p]

    for k in range(steps + 1):
        s, _, p, _ = bufs(k)
        most = s.at[: slots - ROWS_F]
        pltpu.make_async_copy(most, most, fsend.at[k]).wait()
        most = p.at[: slots - ROWS_G]
        pltpu.make_async_copy(most, most, gsend.at[k]).wait()
    for h in range(PARTS):
        sent = wf.at[0, :15, h * PIECE : (h + 1) * PIECE]
        pltpu.make_async_copy(sent, sent, wsend.at[h]).wait()
        pltpu.make_async_copy(sent, sent, csend.at[h]).wait()


def main(floats, place, tokens, goals, weight, at, b):
    slots, width, kv = place.shape[0], tokens.shape[1], b.shape[1]
    chunk = 1024
    steps = width // chunk
    extra = goals.shape[1]
    whole = pl.BlockSpec(memory_space=pltpu.VMEM)
    four = [pltpu.VMEM((slots, extra), BF16), pltpu.VMEM((steps, slots, chunk), BF16)] * 4
    dma = pltpu.SemaphoreType.DMA
    return pl.pallas_call(
        main_kernel,
        out_shape=jax.ShapeDtypeStruct((2, 2, 2, 2, 2, 2, SLAB, 128), F32),
        in_specs=[
            pl.BlockSpec(memory_space=pltpu.SMEM),
            whole,
            whole,
            whole,
            pl.BlockSpec(memory_space=pl.ANY),
            whole,
            whole,
        ],
        out_specs=whole,
        scratch_shapes=[
            *four,
            pltpu.VMEM((2, SIDE * SIDE, *[weight.shape[0], kv // 2]), BF16),
            pltpu.VMEM((2, slots, kv // 2), F32),
            pltpu.VMEM((slots, at.shape[0]), F32),
            pltpu.VMEM(at.shape, F32),
            pltpu.VMEM(b.shape, F32),
            pltpu.VMEM((at.shape[0], 128), F32),
            dma((steps + 1,)),
            dma((steps + 1,)),
            dma((steps + 1,)),
            dma((steps + 1,)),
            dma((PARTS,)),
            dma((PARTS, 16)),
            dma((PARTS,)),
            dma((PARTS, 16)),
            dma((2 * PARTS,)),
        ],
        compiler_params=pltpu.CompilerParams(
            collective_id=1, has_side_effects=True, vmem_limit_bytes=60 << 20
        ),
        name="exchange_and_adapt",
    )(floats, place, tokens, goals, weight, at, b)


CUT = 40


def reduce_kernel(
    s_ref, out_ref, a0, a1, a2, a3, a4, a5, a6, s1, b0, b1, b2, b3, b4, b5, b6, t1, send, recv
):
    y, c, x, z = places()

    def dev(y=y, c=c, x=x, z=z):
        return (y * 2 + c, x * SIDE + z)

    yb, xb, zh = bits(y, c), bits(x, c), z // 2
    yn, xn = sides(y, c), sides(x, c)
    across = dev(c=1 - c)
    over_y = [dev(y=n) for n in yn]
    over_x = [dev(x=n) for n in xn]
    over_z = [dev(z=mirror(z)), dev(z=low(z))]
    partners = [across, *over_y, *over_x, *over_z]
    barrier = pltpu.get_barrier_semaphore()
    for d in partners:
        pl.semaphore_signal(barrier, inc=1, device_id=d, device_id_type=MESH)
    pl.semaphore_wait(barrier, len(partners))

    started = []

    def go(src, dst, to):
        n = len(started)
        d = pltpu.make_async_remote_copy(
            src_ref=src, dst_ref=dst, send_sem=send.at[n], recv_sem=recv.at[n],
            device_id=to, device_id_type=MESH,
        )
        d.start()
        started.append(d)
        return d

    top, low_rows = slice(0, CUT), slice(CUT, SLAB)
    da = go(s_ref.at[1 - c, :, :, :, :, :, top], a0, across)
    db = go(s_ref.at[1 - c, :, :, :, :, :, low_rows], b0, across)

    da.wait_recv()
    s1[...] = s_ref[c, :, :, :, :, :, top] + a0[...]
    da = go(s1.at[1 - yb[0]], a1, over_y[0])
    db.wait_recv()
    t1[...] = s_ref[c, :, :, :, :, :, low_rows] + b0[...]
    db = go(t1.at[:, :, 1 - xb[0]], b1, over_x[0])

    da.wait_recv()
    a1[...] += s1[yb[0]]
    da = go(a1.at[1 - yb[1]], a2, over_y[1])
    db.wait_recv()
    b1[...] += t1[:, :, xb[0]]
    db = go(b1.at[:, :, 1 - xb[1]], b2, over_x[1])

    da.wait_recv()
    a2[...] += a1[yb[1]]
    da = go(a2.at[1 - xb[0]], a3, over_x[0])
    db.wait_recv()
    b2[...] += b1[:, :, xb[1]]
    db = go(b2.at[1 - yb[0]], b3, over_y[0])

    da.wait_recv()
    a3[...] += a2[xb[0]]
    da = go(a3.at[1 - xb[1]], a4, over_x[1])
    db.wait_recv()
    b3[...] += b2[yb[0]]
    db = go(b3.at[1 - yb[1]], b4, over_y[1])

    da.wait_recv()
    a4[...] += a3[xb[1]]
    da = go(a4.at[1 - zh], a5, over_z[0])
    db.wait_recv()
    b4[...] += b3[yb[1]]
    db = go(b4.at[1 - zh], b5, over_z[0])

    da.wait_recv()
    a5[...] += a4[zh]
    da = go(a5, a6, over_z[1])
    db.wait_recv()
    b5[...] += b4[zh]
    db = go(b5, b6, over_z[1])

    da.wait_recv()
    out_ref[top] = a5[...] + a6[...]
    db.wait_recv()
    out_ref[low_rows] = b5[...] + b6[...]
    for d in started:
        d.wait_send()


def reduce(slabs):
    def halves(n):
        two = (2, 2, 2, 2, 2)
        bufs = [pltpu.VMEM((*two[k:], n, 128), F32) for k in (0, 1, 2, 3, 4, 5)]
        return [bufs[0], *bufs[1:], pltpu.VMEM((n, 128), F32), pltpu.VMEM((*two, n, 128), F32)]

    return pl.pallas_call(
        reduce_kernel,
        out_shape=jax.ShapeDtypeStruct((SLAB, 128), F32),
        in_specs=[pl.BlockSpec(memory_space=pltpu.VMEM)],
        out_specs=pl.BlockSpec(memory_space=pltpu.VMEM),
        scratch_shapes=[
            *halves(CUT),
            *halves(SLAB - CUT),
            pltpu.SemaphoreType.DMA((14,)),
            pltpu.SemaphoreType.DMA((14,)),
        ],
        compiler_params=pltpu.CompilerParams(collective_id=0, has_side_effects=True),
        name="reduce_slabs",
    )(slabs)


def body(
    tokens,
    targets,
    row_owner_user,
    device_row_count,
    user_row_cap,
    value_weight,
    adapter_down,
    adapter_up,
    clip_norm_bound,
    down_noise,
    up_noise,
):
    devices = lax.axis_size(BOTH)
    myself = lax.axis_index(BOTH)
    across = lax.axis_size("fsdp")
    per_dev = tokens.shape[0]
    users = user_row_cap.shape[0]
    most = 3 * per_dev // (2 * devices)
    slots = devices * most

    user_of = row_owner_user[:, 0]
    position = jnp.arange(per_dev, dtype=jnp.int32)
    same = (user_of[:, None] == user_of[None, :]) & (position[None, :] < position[:, None])
    rank = jnp.sum(same.astype(jnp.int32), axis=1)
    slot = (user_of % across) * ROWS_F + user_of // across * most + rank
    place = (jnp.arange(slots, dtype=jnp.int32)[:, None] == slot[None, :]).astype(BF16)
    in_use = (position < device_row_count[0]).astype(BF16)
    goals = jnp.concatenate([targets, jnp.broadcast_to(in_use[:, None], (per_dev, 128))], axis=1)
    cap = jnp.sum(jnp.where(jnp.arange(users, dtype=jnp.int32) == myself, user_row_cap, 0))
    bound = clip_norm_bound[0]
    floats = jnp.stack([cap.astype(F32), bound])
    slabs = main(floats, place, tokens, goals, value_weight, adapter_down.T, adapter_up)
    slab = reduce(slabs)
    odd = myself % 2
    mine = jnp.where(odd == 0, slab[:, :64], slab[:, 64:])
    update_a = mine[:ROWS_A].T + bound * down_noise
    update_b = mine[ROWS_A:].T + bound * up_noise
    return update_a, update_b


def solution(mesh):
    in_specs = (
        P(BOTH, None),
        P(BOTH, None),
        P(BOTH, None),
        P(BOTH),
        P(),
        P("fsdp", None),
        P(),
        P(),
        P(),
        P(BOTH, None),
        P(None, BOTH),
    )
    out_specs = (P(BOTH, None), P(None, BOTH))
    return jax.shard_map(
        body, mesh=mesh, in_specs=in_specs, out_specs=out_specs, check_vma=False
    )
```

```python
import functools

import jax
import jax.numpy as jnp
from jax import lax
from jax.experimental import pallas as pl
from jax.experimental.pallas import tpu as pltpu
from jax.sharding import PartitionSpec as P

STEPS = 2
BOTH = ("grp", "fsdp")
MESH = pl.DeviceIdType.MESH
scale = 2.0
rate = 0.05
epsilon = 1e-06
F32 = jnp.float32
BF16 = jnp.bfloat16
SIDE = 4
ROWS_A = 64
SLAB = 72


def mm(a, b, ca, cb):
    return lax.dot_general(a, b, (((ca,), (cb,)), ((), ())), preferred_element_type=F32)


def slab_place(p):
    y, c, x, zh = p // 16, p // 8 % 2, p // 2 % 4, p % 2
    def code(i):
        u, v = i // 2, (i ^ (i // 2)) & 1
        return (v, u) if c == 0 else (u, v)
    return (c, *code(y), *code(x), zh)


def places():
    g, f = lax.axis_index("grp"), lax.axis_index("fsdp")
    return g // 2, g % 2, f // SIDE, f % SIDE


def low(i):
    return i + 1 - 2 * (i % 2)


def mirror(i):
    return 3 - i


def bits(i, c):
    u = i // 2
    v = (i + i // 2) % 2
    return c * u + (1 - c) * v, c * v + (1 - c) * u


def sides(i, c):
    return c * mirror(i) + (1 - c) * low(i), c * low(i) + (1 - c) * mirror(i)


CUT = 40


def sum_slabs(s_ref, out_ref, a0, a1, a2, a3, a4, a5, a6, s1, b0, b1, b2, b3, b4, b5, b6, t1, send, recv):
    y, c, x, z = places()

    def dev(y=y, c=c, x=x, z=z):
        return (y * 2 + c, x * SIDE + z)

    yb, xb, zh = bits(y, c), bits(x, c), z // 2
    yn, xn = sides(y, c), sides(x, c)
    across = dev(c=1 - c)
    over_y = [dev(y=n) for n in yn]
    over_x = [dev(x=n) for n in xn]
    over_z = [dev(z=mirror(z)), dev(z=low(z))]
    started = []

    def go(src, dst, to):
        n = len(started)
        d = pltpu.make_async_remote_copy(
            src_ref=src, dst_ref=dst, send_sem=send.at[n], recv_sem=recv.at[n],
            device_id=to, device_id_type=MESH,
        )
        d.start()
        started.append(d)
        return d

    top, low_rows = slice(0, CUT), slice(CUT, SLAB)
    da = go(s_ref.at[1 - c, :, :, :, :, :, top], a0, across)
    db = go(s_ref.at[1 - c, :, :, :, :, :, low_rows], b0, across)

    da.wait_recv()
    s1[...] = s_ref[c, :, :, :, :, :, top] + a0[...]
    da = go(s1.at[1 - yb[0]], a1, over_y[0])
    db.wait_recv()
    t1[...] = s_ref[c, :, :, :, :, :, low_rows] + b0[...]
    db = go(t1.at[:, :, 1 - xb[0]], b1, over_x[0])

    da.wait_recv()
    a1[...] += s1[yb[0]]
    da = go(a1.at[1 - yb[1]], a2, over_y[1])
    db.wait_recv()
    b1[...] += t1[:, :, xb[0]]
    db = go(b1.at[:, :, 1 - xb[1]], b2, over_x[1])

    da.wait_recv()
    a2[...] += a1[yb[1]]
    da = go(a2.at[1 - xb[0]], a3, over_x[0])
    db.wait_recv()
    b2[...] += b1[:, :, xb[1]]
    db = go(b2.at[1 - yb[0]], b3, over_y[0])

    da.wait_recv()
    a3[...] += a2[xb[0]]
    da = go(a3.at[1 - xb[1]], a4, over_x[1])
    db.wait_recv()
    b3[...] += b2[yb[0]]
    db = go(b3.at[1 - yb[1]], b4, over_y[1])

    da.wait_recv()
    a4[...] += a3[xb[1]]
    da = go(a4.at[1 - zh], a5, over_z[0])
    db.wait_recv()
    b4[...] += b3[yb[1]]
    db = go(b4.at[1 - zh], b5, over_z[0])

    da.wait_recv()
    a5[...] += a4[zh]
    da = go(a5, a6, over_z[1])
    db.wait_recv()
    b5[...] += b4[zh]
    db = go(b5, b6, over_z[1])

    da.wait_recv()
    out_ref[top] = a5[...] + a6[...]
    db.wait_recv()
    out_ref[low_rows] = b5[...] + b6[...]
    for d in started:
        d.wait_send()


ROWS_F = 16
ROWS_G = 32
AHEAD = 2
PARTS = 2
PIECE = 256
ORDER = [(1, 0), (0, 1), (3, 0), (0, 3), (1, 1), (3, 3), (1, 3), (3, 1), (2, 0), (0, 2), (2, 1), (1, 2), (2, 3), (3, 2), (2, 2)]


def flip(i, by_low, by_mirror):
    i = i + by_low * (1 - 2 * (i % 2))
    return i + by_mirror * (3 - 2 * i)


def piece(i, h, a, b):
    i0, i1, i2, i3 = i % 2, i // 2 % 2, i // 4 % 2, i // 8
    if h == 1:
        i0, i1, i2, i3 = i1, i0, i3, i2
    return flip(a, i0, i1), flip(b, i2, i3)


def main_kernel(
    cap_ref, count_ref, bound_ref, user_ref, tok_ref, tgt_ref, w_ref, down_ref, b_ref, out_ref,
    place_ref, at_ref, st, sx, rt, rx, pt, px, gt, gx, wf, acc, hid, a1, bcur, sq, slabs,
    a_bufs, b_bufs, fsend, frecv, gsend, grecv, wsend, wrecv, csend, crecv, local, ssend, srecv,
):
    y, c, x, z = places()
    g, f = y * 2 + c, x * SIDE + z
    a, b = (1 - c) * x + c * z, (1 - c) * z + c * x
    width = tok_ref.shape[1]
    kv = b_ref.shape[1]
    chunk = sx.shape[2]
    steps = width // chunk
    slots = st.shape[0]
    half = kv // 2

    def column(pos, core):
        return pos[0] * (SIDE - 3 * core) + pos[1] * (1 + 3 * core)

    f_peers = []
    for dx, dz in ORDER:
        f_peers.append((x + dx) % SIDE * SIDE + (z + dz) % SIDE)
    g_peers = []
    for dy, dc in [(1, 0), (3, 1), (3, 0), (1, 1), (2, 0), (2, 1), (0, 1)]:
        g_peers.append((y + dy) % SIDE * 2 + (c + dc) % 2)

    barrier = pltpu.get_barrier_semaphore()
    for to in f_peers:
        pl.semaphore_signal(barrier, inc=1, device_id=(g, to), device_id_type=MESH)
    for to in g_peers:
        pl.semaphore_signal(barrier, inc=1, device_id=(to, f), device_id_type=MESH)

    keep = []
    for h in range(PARTS):
        rows = slice(h * PIECE, (h + 1) * PIECE)
        for n in range(2):
            keep.append(
                pltpu.make_async_copy(w_ref.at[rows, n * half : (n + 1) * half], wf.at[n, f, rows], local.at[2 * h + n])
            )
            keep[-1].start()

    user = user_ref[...]
    per = user.shape[0]
    u_i = lax.broadcasted_iota(jnp.int32, (per, per), 0)
    v_i = lax.broadcasted_iota(jnp.int32, (per, per), 1)
    lane = lax.broadcasted_iota(jnp.int32, (per, 128), 1)
    named = jnp.where(lane == user, 1.0, 0.0)
    below = jnp.where(v_i < u_i, 1.0, 0.0).astype(BF16)
    rank = jnp.sum(mm(below, named.astype(BF16), 1, 0) * named, axis=1, keepdims=True).astype(jnp.int32)
    slot = (user & 15) * ROWS_F + (user >> 4) * 2 + rank
    s_i = lax.broadcasted_iota(jnp.int32, (per, slots), 1)
    place_ref[...] = jnp.where(s_i == slot, 1.0, 0.0).T.astype(BF16)
    count = count_ref[0]
    flags = jnp.where(lax.broadcasted_iota(jnp.int32, (per, 128), 0) < count, 1.0, 0.0).astype(BF16)
    place = place_ref[...]
    n_i = lax.broadcasted_iota(jnp.int32, (slots, slots), 0)
    o_i = lax.broadcasted_iota(jnp.int32, (slots, slots), 1)
    old = ((n_i >> 1) & 15) * 16 + (n_i >> 5) * 2 + (n_i & 1)
    turn = jnp.where(o_i == old, 1.0, 0.0).astype(BF16)

    def bufs(k):
        if k == 0:
            return st, rt, pt, gt
        return sx.at[k - 1], rx.at[k - 1], px.at[k - 1], gx.at[k - 1]

    def rows_f(i):
        return pl.ds(pl.multiple_of(i * ROWS_F, ROWS_F), ROWS_F)

    def rows_g(i):
        return pl.ds(pl.multiple_of(i * ROWS_G, ROWS_G), ROWS_G)

    def place_rows(k):
        s = bufs(k)[0]
        if k == 0:
            s[:, :kv] = mm(place, tgt_ref[...], 1, 0).astype(BF16)
            s[:, kv:] = mm(place, flags, 1, 0).astype(BF16)
        else:
            s[...] = mm(place, tok_ref[:, (k - 1) * chunk : k * chunk], 1, 0).astype(BF16)

    def start_f(k):
        s, r, _, _ = bufs(k)
        for to in f_peers:
            pltpu.make_async_remote_copy(
                src_ref=s.at[rows_f(to)], dst_ref=r.at[rows_f(f)], send_sem=fsend.at[k], recv_sem=frecv.at[k],
                device_id=(g, to), device_id_type=MESH,
            ).start()
        r[rows_f(f), :] = s[rows_f(f), :]

    def turn_rows(k):
        _, r, p, q = bufs(k)
        most = r.at[: slots - ROWS_F]
        pltpu.make_async_copy(most, most, frecv.at[k]).wait()
        p[...] = mm(turn, r[...], 1, 0).astype(BF16)
        for to in g_peers:
            pltpu.make_async_remote_copy(
                src_ref=p.at[rows_g(to)], dst_ref=q.at[rows_g(g)], send_sem=gsend.at[k], recv_sem=grecv.at[k],
                device_id=(to, f), device_id_type=MESH,
            ).start()
        q[rows_g(g), :] = p[rows_g(g), :]

    def end_g(k):
        q = bufs(k)[3]
        most = q.at[: slots - ROWS_G]
        pltpu.make_async_copy(most, most, grecv.at[k]).wait()

    def weight(i, h):
        return wf.at[c, column(piece(i, h, a, b), c), h * PIECE : (h + 1) * PIECE]

    def pass_on(i, h):
        level = i.bit_length()
        to_ref = weight(i, h)
        if i == 0:
            src = w_ref.at[h * PIECE : (h + 1) * PIECE, pl.ds(pl.multiple_of(c * half, half), half)]
        else:
            src = to_ref
            pltpu.make_async_copy(src, src, wrecv.at[h, i]).wait()
            swap(i, h)
        for n in range(level, 4):
            to = column(piece(1 << n, h, a, b), c)
            pltpu.make_async_remote_copy(
                src_ref=src, dst_ref=to_ref, send_sem=wsend.at[h], recv_sem=wrecv.at[h, (1 << n) + i],
                device_id=(g, to), device_id_type=MESH,
            ).start()

    def swap(i, h):
        ref = weight(i, h)
        pltpu.make_async_remote_copy(
            src_ref=ref, dst_ref=ref, send_sem=csend.at[h], recv_sem=crecv.at[h, i],
            device_id=(y * 2 + 1 - c, f), device_id_type=MESH,
        ).start()

    def other_column(i, h):
        return column(piece(i, h, b, a), 1 - c)

    def add(n, col, h):
        per = chunk // (PARTS * PIECE)
        x_cols = gx[col // per, :, pl.ds(pl.multiple_of(col % per * (PARTS * PIECE) + h * PIECE, PIECE), PIECE)]
        acc[n] += mm(x_cols, wf[n, col, h * PIECE : (h + 1) * PIECE, :], 1, 0)

    place_rows(0)
    pl.semaphore_wait(barrier, len(f_peers) + len(g_peers))
    start_f(0)
    place_rows(1)
    start_f(1)
    acc[...] = jnp.zeros_like(acc)
    hid[...] = jnp.zeros_like(hid)
    for k in range(steps):
        cols = slice(k * chunk, (k + 1) * chunk)
        at_ref[:, cols] = down_ref[cols, :].astype(F32).T.astype(BF16)
    todo = {1: [0], 6: [1], 8: [2, 3], 10: [4, 5, 6, 7]}
    for k in range(1, steps + 1 + AHEAD):
        if 1 < k <= steps:
            place_rows(k)
            start_f(k)
        if k >= AHEAD:
            turn_rows(k - AHEAD)
        for i in todo.get(k, []):
            for h in range(PARTS):
                pass_on(i, h)

    end_g(0)
    for k in range(1, steps + 1):
        end_g(k)
        hid[...] += mm(gx[k - 1], at_ref[:, (k - 1) * chunk : k * chunk], 1, 1)
    for d in keep:
        d.wait()
    for n in range(2):
        for h in range(PARTS):
            add(n, f, h)

    @pl.loop(1, 8)
    def _(i):
        for h in range(PARTS):
            add(c, column(piece(i, h, a, b), c), h)
            col = other_column(i, h)
            ref = wf.at[1 - c, col, h * PIECE : (h + 1) * PIECE]
            pltpu.make_async_copy(ref, ref, crecv.at[h, i]).wait()
            add(1 - c, col, h)

    @pl.loop(8, 16)
    def _(i):
        for h in range(PARTS):
            ref = weight(i, h)
            pltpu.make_async_copy(ref, ref, wrecv.at[h, i]).wait()
            swap(i, h)
            add(c, column(piece(i, h, a, b), c), h)

    @pl.loop(8, 16)
    def _(i):
        for h in range(PARTS):
            col = other_column(i, h)
            ref = wf.at[1 - c, col, h * PIECE : (h + 1) * PIECE]
            pltpu.make_async_copy(ref, ref, crecv.at[h, i]).wait()
            add(1 - c, col, h)

    cap, bound = cap_ref[g * SIDE * SIDE + f].astype(F32), bound_ref[0]
    used = gt[:, kv:]
    before = jnp.where(o_i < n_i, 1.0, 0.0).astype(BF16)
    earlier = mm(before, used, 1, 0)
    live = jnp.where((used.astype(F32) > 0.5) & (earlier < cap), 1.0 / cap, 0.0)
    live = jnp.concatenate([live] * (kv // live.shape[1]), axis=1)
    base = jnp.concatenate([acc[0], acc[1]], axis=1) - gt[:, :kv].astype(F32)

    def part(k):
        return pl.ds(pl.multiple_of(k * chunk, chunk), chunk)

    def errors(h, b16):
        r = (live * (base + scale * mm(h, b16, 1, 0))).astype(BF16)
        return mm(r, b16, 1, 1).astype(BF16), scale * mm(h, r, 0, 0)

    b0 = b_ref[...]
    back, grad_b = errors(hid[...].astype(BF16), b0)
    bcur[...] = b0.astype(F32) - rate * grad_b
    hid[...] = jnp.zeros_like(hid)

    @pl.loop(0, steps)
    def _(k):
        rows = gx[k]
        now = at_ref[:, part(k)].astype(F32) - rate * (scale * mm(back, rows, 0, 0))
        a1[:, part(k)] = now
        hid[...] += mm(rows, now.astype(BF16), 1, 1)

    back2, grad_b2 = errors(hid[...].astype(BF16), bcur[...].astype(BF16))
    delta_b = (bcur[...] - rate * grad_b2) - b0.astype(F32)
    sq[...] = jnp.zeros_like(sq)

    @pl.loop(0, steps)
    def _(k):
        d = (a1[:, part(k)] - rate * (scale * mm(back2, gx[k], 0, 0))) - at_ref[:, part(k)].astype(F32)
        a1[:, part(k)] = d
        sq[...] += jnp.sum((d * d).reshape(d.shape[0], chunk // 128, 128), axis=1)

    total = jnp.sum(sq[...]) + jnp.sum(delta_b * delta_b)
    factor = jnp.minimum(1.0, bound / jnp.sqrt(jnp.broadcast_to(total, (8, 128)) + epsilon))
    fa = jnp.concatenate([factor] * (ROWS_A // 8), axis=0)
    pairs = width // 128
    bt = (delta_b * factor[:1, :1]).T.reshape(pairs, 16, ROWS_A)
    packed = jnp.concatenate([bt[:, :8, :], bt[:, 8:, :]], axis=2)
    for p in range(pairs):
        spot = slab_place(p)
        slabs[(*spot, slice(0, ROWS_A), slice(None))] = fa * a1[:, p * 128 : (p + 1) * 128]
        slabs[(*spot, slice(ROWS_A, SLAB), slice(None))] = packed[p]
    sum_slabs(slabs, out_ref, *a_bufs, *b_bufs, ssend, srecv)

    for k in range(steps + 1):
        s, _, p, _ = bufs(k)
        most = s.at[: slots - ROWS_F]
        pltpu.make_async_copy(most, most, fsend.at[k]).wait()
        most = p.at[: slots - ROWS_G]
        pltpu.make_async_copy(most, most, gsend.at[k]).wait()
    for h in range(PARTS):
        sent = wf.at[0, :15, h * PIECE : (h + 1) * PIECE]
        pltpu.make_async_copy(sent, sent, wsend.at[h]).wait()
        pltpu.make_async_copy(sent, sent, csend.at[h]).wait()


def main(caps, count, bound, user, tokens, goals, weight, down, b):
    width, kv = tokens.shape[1], b.shape[1]
    slots = ROWS_F * SIDE * SIDE
    chunk = 1024
    steps = width // chunk
    extra = kv + 128
    whole = pl.BlockSpec(memory_space=pltpu.VMEM)
    scalars = pl.BlockSpec(memory_space=pltpu.SMEM)
    four = [pltpu.VMEM((slots, extra), BF16), pltpu.VMEM((steps, slots, chunk), BF16)] * 4
    dma = pltpu.SemaphoreType.DMA

    def halves(n):
        two = (2, 2, 2, 2, 2)
        bufs = [pltpu.VMEM((*two[k:], n, 128), F32) for k in range(6)]
        return (*bufs, pltpu.VMEM((n, 128), F32), pltpu.VMEM((*two, n, 128), F32))

    return pl.pallas_call(
        main_kernel,
        out_shape=jax.ShapeDtypeStruct((SLAB, 128), F32),
        in_specs=[scalars] * 3 + [whole] * 3 + [pl.BlockSpec(memory_space=pl.ANY)] + [whole] * 2,
        out_specs=whole,
        scratch_shapes=[
            pltpu.VMEM((slots, tokens.shape[0]), BF16),
            pltpu.VMEM((down.shape[1], width), BF16),
            *four,
            pltpu.VMEM((2, SIDE * SIDE, weight.shape[0], kv // 2), BF16),
            pltpu.VMEM((2, slots, kv // 2), F32),
            pltpu.VMEM((slots, down.shape[1]), F32),
            pltpu.VMEM((down.shape[1], width), F32),
            pltpu.VMEM(b.shape, F32),
            pltpu.VMEM((down.shape[1], 128), F32),
            pltpu.VMEM((2, 2, 2, 2, 2, 2, SLAB, 128), F32),
            halves(CUT),
            halves(SLAB - CUT),
            dma((steps + 1,)),
            dma((steps + 1,)),
            dma((steps + 1,)),
            dma((steps + 1,)),
            dma((PARTS,)),
            dma((PARTS, 16)),
            dma((PARTS,)),
            dma((PARTS, 16)),
            dma((2 * PARTS,)),
            dma((14,)),
            dma((14,)),
        ],
        compiler_params=pltpu.CompilerParams(
            collective_id=0, has_side_effects=True, vmem_limit_bytes=62 << 20
        ),
        name="exchange_and_adapt",
    )(caps, count, bound, user, tokens, goals, weight, down, b)


def body(
    tokens,
    targets,
    row_owner_user,
    device_row_count,
    user_row_cap,
    value_weight,
    adapter_down,
    adapter_up,
    clip_norm_bound,
    down_noise,
    up_noise,
):
    myself = lax.axis_index(BOTH)
    bound = clip_norm_bound[0]
    slab = main(
        user_row_cap, device_row_count, clip_norm_bound, row_owner_user, tokens, targets, value_weight,
        adapter_down, adapter_up,
    )
    odd = myself % 2
    mine = jnp.where(odd == 0, slab[:, :64], slab[:, 64:])
    update_a = mine[:ROWS_A].T + bound * down_noise
    update_b = mine[ROWS_A:].T + bound * up_noise
    return update_a, update_b


def solution(mesh):
    in_specs = (
        P(BOTH, None),
        P(BOTH, None),
        P(BOTH, None),
        P(BOTH),
        P(),
        P("fsdp", None),
        P(),
        P(),
        P(),
        P(BOTH, None),
        P(None, BOTH),
    )
    out_specs = (P(BOTH, None), P(None, BOTH))
    return jax.shard_map(
        body, mesh=mesh, in_specs=in_specs, out_specs=out_specs, check_vma=False
    )
```

```python
import functools

import jax
import jax.numpy as jnp
from jax import lax
from jax.experimental import pallas as pl
from jax.experimental.pallas import tpu as pltpu
from jax.sharding import PartitionSpec as P

STEPS = 2
BOTH = ("grp", "fsdp")
MESH = pl.DeviceIdType.MESH
scale = 2.0
rate = 0.05
epsilon = 1e-06
F32 = jnp.float32
BF16 = jnp.bfloat16
SIDE = 4
ROWS_A = 64
SLAB = 72


def mm(a, b, ca, cb):
    return lax.dot_general(a, b, (((ca,), (cb,)), ((), ())), preferred_element_type=F32)


def places():
    g, f = lax.axis_index("grp"), lax.axis_index("fsdp")
    return g // 2, g % 2, f // SIDE, f % SIDE


def low(i):
    return i + 1 - 2 * (i % 2)


def mirror(i):
    return 3 - i


def bits(i, c):
    u = i // 2
    v = (i + i // 2) % 2
    return c * u + (1 - c) * v, c * v + (1 - c) * u


def sides(i, c):
    return c * mirror(i) + (1 - c) * low(i), c * low(i) + (1 - c) * mirror(i)


ROUTES = [
    ("y1", "y2", "x1", "x2", "ring"),
    ("x1", "x2", "y1", "y2", "ring"),
    ("z", "y1", "y2", "x1", "x2", "pair"),
]
THIRD = SLAB // len(ROUTES)
FIRST_SEM = SIDE + 1
SUM_SEMS = FIRST_SEM + sum(len(r) + 2 * ("ring" in r) for r in ROUTES)


def sum_slabs(kept, taken, factor, far, chains, send, recv):
    y, c, x, z = places()

    def dev(y=y, c=c, x=x, z=z):
        return (y * 2 + c, x * SIDE + z)

    yb, xb, yn, xn = bits(y, c), bits(x, c), sides(y, c), sides(x, c)
    bit = {"y1": yb[0], "y2": yb[1], "x1": xb[0], "x2": xb[1], "z": z // 2}
    to = {
        "y1": dev(y=yn[0]),
        "y2": dev(y=yn[1]),
        "x1": dev(x=xn[0]),
        "x2": dev(x=xn[1]),
        "z": dev(z=mirror(z)),
        "pair": dev(z=low(z)),
    }
    started = []

    def go(src, dst, device):
        n = FIRST_SEM + len(started)
        d = pltpu.make_async_remote_copy(
            src_ref=src, dst_ref=dst, send_sem=send.at[n], recv_sem=recv.at[n],
            device_id=device, device_id_type=MESH,
        )
        d.start()
        started.append(d)
        return d

    near = jnp.concatenate([factor] * (THIRD // 8), axis=0)
    away = jnp.concatenate([far] * (THIRD // 8), axis=0)
    now, dims, flying = [], [], []

    def at(ref, left, dim, i):
        return ref.at[(slice(None),) * left.index(dim) + (i,)]

    def launch(n, step):
        route, bufs = ROUTES[n], chains[n]
        dim, ref, left = route[step], now[n], dims[n]
        into = bufs[step + 1]
        if dim == "ring":
            flying[n] = [
                go(ref.at[(z + j) % SIDE // 2], into.at[j - 1], dev(z=(z + j) % SIDE)) for j in range(1, SIDE)
            ]
        elif dim == "pair":
            flying[n] = [go(ref, into, to[dim])]
        else:
            flying[n] = [go(at(ref, left, dim, 1 - bit[dim]), into, to[dim])]

    def land(n, step):
        route, bufs = ROUTES[n], chains[n]
        dim, ref, left = route[step], now[n], dims[n]
        into = bufs[step + 1]
        for d in flying[n]:
            d.wait_recv()
        if dim == "ring":
            return ref[z // 2] + into[0] + into[1] + into[2]
        if dim == "pair":
            return ref[...] + into[...]
        into[...] += at(ref, left, dim, bit[dim])[...]
        now[n] = into
        dims[n] = [v for v in left if v != dim]
        return None

    results = [None] * len(ROUTES)
    for n in range(len(ROUTES)):
        rows = slice(n * THIRD, (n + 1) * THIRD)
        ref = chains[n][0]
        ref[...] = near * kept[:, :, :, :, :, rows] + away * taken[:, :, :, :, :, rows]
        now.append(ref)
        dims.append(["y1", "y2", "x1", "x2", "z"])
        flying.append(None)
        launch(n, 0)
    for step in range(max(len(r) for r in ROUTES)):
        for n, route in enumerate(ROUTES):
            if step < len(route):
                results[n] = land(n, step)
                if step + 1 < len(route):
                    launch(n, step + 1)
    for d in started:
        d.wait_send()
    return jnp.concatenate(results, axis=0)


ROWS_F = 16
ROWS_G = 32
AHEAD = 2
PARTS = 2
PIECE = 256
ORDER = [(1, 0), (0, 1), (3, 0), (0, 3), (1, 1), (3, 3), (1, 3), (3, 1), (2, 0), (0, 2), (2, 1), (1, 2), (2, 3), (3, 2), (2, 2)]


def flip(i, by_low, by_mirror):
    i = i + by_low * (1 - 2 * (i % 2))
    return i + by_mirror * (3 - 2 * i)


def piece(i, h, a, b):
    i0, i1, i2, i3 = i % 2, i // 2 % 2, i // 4 % 2, i // 8
    if h == 1:
        i0, i1, i2, i3 = i1, i0, i3, i2
    return flip(a, i0, i1), flip(b, i2, i3)


def main_kernel(
    cap_ref, count_ref, bound_ref, user_ref, tok_ref, tgt_ref, w_ref, at_ref, b_ref, na_ref, nb_ref,
    oa_ref, ob_ref, place_ref, st, sx, rt, rx, pt, px, gt, gx, wf, acc, hid, a1, bcur, sq,
    given, kept, taken, packed, own_factor, far_factor, chains, fsend, frecv, gsend, grecv, wsend, wrecv, csend, crecv, local, ssend, srecv,
):
    y, c, x, z = places()
    g, f = y * 2 + c, x * SIDE + z
    a, b = (1 - c) * x + c * z, (1 - c) * z + c * x
    width = tok_ref.shape[1]
    kv = b_ref.shape[1]
    chunk = sx.shape[2]
    steps = width // chunk
    slots = st.shape[0]
    half = kv // 2

    def column(pos, core):
        return pos[0] * (SIDE - 3 * core) + pos[1] * (1 + 3 * core)

    f_peers = []
    for dx, dz in ORDER:
        f_peers.append((x + dx) % SIDE * SIDE + (z + dz) % SIDE)
    g_peers = []
    for dy, dc in [(1, 0), (3, 1), (3, 0), (1, 1), (2, 0), (2, 1), (0, 1)]:
        g_peers.append((y + dy) % SIDE * 2 + (c + dc) % 2)

    barrier = pltpu.get_barrier_semaphore()
    for to in f_peers:
        pl.semaphore_signal(barrier, inc=1, device_id=(g, to), device_id_type=MESH)
    for to in g_peers:
        pl.semaphore_signal(barrier, inc=1, device_id=(to, f), device_id_type=MESH)

    keep = []
    for h in range(PARTS):
        rows = slice(h * PIECE, (h + 1) * PIECE)
        for n in range(2):
            keep.append(
                pltpu.make_async_copy(w_ref.at[rows, n * half : (n + 1) * half], wf.at[n, f, rows], local.at[2 * h + n])
            )
            keep[-1].start()

    user = user_ref[...]
    per = user.shape[1]
    u_i = lax.broadcasted_iota(jnp.int32, (per, per), 0)
    v_i = lax.broadcasted_iota(jnp.int32, (per, per), 1)
    named = jnp.where(lax.broadcasted_iota(jnp.int32, (128, per), 0) == user, 1.0, 0.0)
    above = jnp.where(u_i < v_i, 1.0, 0.0).astype(BF16)
    rank = jnp.sum(mm(named.astype(BF16), above, 1, 0) * named, axis=0, keepdims=True).astype(jnp.int32)
    slot = (user & 15) * ROWS_F + (user >> 4) * 2 + rank
    place_ref[...] = jnp.where(lax.broadcasted_iota(jnp.int32, (slots, per), 0) == slot, 1.0, 0.0).astype(BF16)
    count = count_ref[0]
    flags = jnp.where(lax.broadcasted_iota(jnp.int32, (per, 128), 0) < count, 1.0, 0.0).astype(BF16)
    place = place_ref[...]
    n_i = lax.broadcasted_iota(jnp.int32, (slots, slots), 0)
    o_i = lax.broadcasted_iota(jnp.int32, (slots, slots), 1)
    old = ((n_i >> 1) & 15) * 16 + (n_i >> 5) * 2 + (n_i & 1)
    turn = jnp.where(o_i == old, 1.0, 0.0).astype(BF16)

    def bufs(k):
        if k == 0:
            return st, rt, pt, gt
        return sx.at[k - 1], rx.at[k - 1], px.at[k - 1], gx.at[k - 1]

    def rows_f(i):
        return pl.ds(pl.multiple_of(i * ROWS_F, ROWS_F), ROWS_F)

    def rows_g(i):
        return pl.ds(pl.multiple_of(i * ROWS_G, ROWS_G), ROWS_G)

    def place_rows(k):
        s = bufs(k)[0]
        if k == 0:
            s[:, :kv] = mm(place, tgt_ref[...], 1, 0).astype(BF16)
            s[:, kv:] = mm(place, flags, 1, 0).astype(BF16)
        else:
            s[...] = mm(place, tok_ref[:, (k - 1) * chunk : k * chunk], 1, 0).astype(BF16)

    def start_f(k):
        s, r, _, _ = bufs(k)
        for to in f_peers:
            pltpu.make_async_remote_copy(
                src_ref=s.at[rows_f(to)], dst_ref=r.at[rows_f(f)], send_sem=fsend.at[k], recv_sem=frecv.at[k],
                device_id=(g, to), device_id_type=MESH,
            ).start()
        r[rows_f(f), :] = s[rows_f(f), :]

    def turn_rows(k):
        _, r, p, q = bufs(k)
        most = r.at[: slots - ROWS_F]
        pltpu.make_async_copy(most, most, frecv.at[k]).wait()
        p[...] = mm(turn, r[...], 1, 0).astype(BF16)
        for to in g_peers:
            pltpu.make_async_remote_copy(
                src_ref=p.at[rows_g(to)], dst_ref=q.at[rows_g(g)], send_sem=gsend.at[k], recv_sem=grecv.at[k],
                device_id=(to, f), device_id_type=MESH,
            ).start()
        q[rows_g(g), :] = p[rows_g(g), :]

    def end_g(k):
        q = bufs(k)[3]
        most = q.at[: slots - ROWS_G]
        pltpu.make_async_copy(most, most, grecv.at[k]).wait()

    def weight(i, h):
        return wf.at[c, column(piece(i, h, a, b), c), h * PIECE : (h + 1) * PIECE]

    def pass_on(i, h):
        level = i.bit_length()
        to_ref = weight(i, h)
        if i == 0:
            src = w_ref.at[h * PIECE : (h + 1) * PIECE, pl.ds(pl.multiple_of(c * half, half), half)]
        else:
            src = to_ref
            pltpu.make_async_copy(src, src, wrecv.at[h, i]).wait()
            swap(i, h)
        for n in range(level, 4):
            to = column(piece(1 << n, h, a, b), c)
            pltpu.make_async_remote_copy(
                src_ref=src, dst_ref=to_ref, send_sem=wsend.at[h], recv_sem=wrecv.at[h, (1 << n) + i],
                device_id=(g, to), device_id_type=MESH,
            ).start()

    def swap(i, h):
        ref = weight(i, h)
        pltpu.make_async_remote_copy(
            src_ref=ref, dst_ref=ref, send_sem=csend.at[h], recv_sem=crecv.at[h, i],
            device_id=(y * 2 + 1 - c, f), device_id_type=MESH,
        ).start()

    def other_column(i, h):
        return column(piece(i, h, b, a), 1 - c)

    def add(n, col, h):
        per = chunk // (PARTS * PIECE)
        x_cols = gx[col // per, :, pl.ds(pl.multiple_of(col % per * (PARTS * PIECE) + h * PIECE, PIECE), PIECE)]
        acc[n] += mm(x_cols, wf[n, col, h * PIECE : (h + 1) * PIECE, :], 1, 0)

    place_rows(0)
    pl.semaphore_wait(barrier, len(f_peers) + len(g_peers))
    start_f(0)
    place_rows(1)
    start_f(1)
    acc[...] = jnp.zeros_like(acc)
    hid[...] = jnp.zeros_like(hid)
    todo = {1: [0], 6: [1], 8: [2, 3], 10: [4, 5, 6, 7]}
    for k in range(1, steps + 1 + AHEAD):
        if 1 < k <= steps:
            place_rows(k)
            start_f(k)
        if k >= AHEAD:
            turn_rows(k - AHEAD)
        for i in todo.get(k, []):
            for h in range(PARTS):
                pass_on(i, h)

    end_g(0)
    for k in range(1, steps + 1):
        end_g(k)
        hid[...] += mm(gx[k - 1], at_ref[:, (k - 1) * chunk : k * chunk], 1, 1)
    for d in keep:
        d.wait()
    for n in range(2):
        for h in range(PARTS):
            add(n, f, h)

    @pl.loop(1, 8)
    def _(i):
        for h in range(PARTS):
            add(c, column(piece(i, h, a, b), c), h)
            col = other_column(i, h)
            ref = wf.at[1 - c, col, h * PIECE : (h + 1) * PIECE]
            pltpu.make_async_copy(ref, ref, crecv.at[h, i]).wait()
            add(1 - c, col, h)

    @pl.loop(8, 16)
    def _(i):
        for h in range(PARTS):
            ref = weight(i, h)
            pltpu.make_async_copy(ref, ref, wrecv.at[h, i]).wait()
            swap(i, h)
            add(c, column(piece(i, h, a, b), c), h)

    @pl.loop(8, 16)
    def _(i):
        for h in range(PARTS):
            col = other_column(i, h)
            ref = wf.at[1 - c, col, h * PIECE : (h + 1) * PIECE]
            pltpu.make_async_copy(ref, ref, crecv.at[h, i]).wait()
            add(1 - c, col, h)

    cap, bound = cap_ref[g * SIDE * SIDE + f].astype(F32), bound_ref[0]
    used = gt[:, kv:]
    before = jnp.where(o_i < n_i, 1.0, 0.0).astype(BF16)
    earlier = mm(before, used, 1, 0)
    live = jnp.where((used.astype(F32) > 0.5) & (earlier < cap), 1.0 / cap, 0.0)
    live = jnp.concatenate([live] * (kv // live.shape[1]), axis=1)
    base = jnp.concatenate([acc[0], acc[1]], axis=1) - gt[:, :kv].astype(F32)

    def part(k):
        return pl.ds(pl.multiple_of(k * chunk, chunk), chunk)

    def errors(h, b16):
        r = (live * (base + scale * mm(h, b16, 1, 0))).astype(BF16)
        return mm(r, b16, 1, 1).astype(BF16), scale * mm(h, r, 0, 0)

    b0 = b_ref[...]
    back, grad_b = errors(hid[...].astype(BF16), b0)
    bcur[...] = b0.astype(F32) - rate * grad_b
    hid[...] = jnp.zeros_like(hid)

    @pl.loop(0, steps)
    def _(k):
        rows = gx[k]
        now = at_ref[:, part(k)].astype(F32) - rate * (scale * mm(back, rows, 0, 0))
        a1[:, part(k)] = now
        hid[...] += mm(rows, now.astype(BF16), 1, 1)

    back2, grad_b2 = errors(hid[...].astype(BF16), bcur[...].astype(BF16))
    delta_b = (bcur[...] - rate * grad_b2) - b0.astype(F32)
    sq[...] = jnp.zeros_like(sq)

    bt = delta_b.T.reshape(width // 128, 16, ROWS_A)
    packed[...] = jnp.concatenate([bt[:, :8, :], bt[:, 8:, :]], axis=2)
    other_core = (y * 2 + 1 - c, f)

    def to_core(src, dst, n):
        return pltpu.make_async_remote_copy(
            src_ref=src, dst_ref=dst, send_sem=ssend.at[n], recv_sem=srecv.at[n],
            device_id=other_core, device_id_type=MESH,
        )

    first = []
    for to_far in (True, False):
        core = 1 - c if to_far else c
        slabs = given if to_far else kept
        for yy in range(SIDE):
            k = yy * 2 + core
            d = (a1[:, part(k)] - rate * (scale * mm(back2, gx[k], 0, 0))) - at_ref[:, part(k)].astype(F32)
            sq[...] += jnp.sum((d * d).reshape(d.shape[0], chunk // 128, 128), axis=1)
            y1, y2 = bits(yy, core)
            for p in range(chunk // 128):
                x1, x2 = bits(p // 2, core)
                slabs[y1, y2, x1, x2, p % 2, :ROWS_A, :] = d[:, p * 128 : (p + 1) * 128]
                slabs[y1, y2, x1, x2, p % 2, ROWS_A:, :] = packed[k * (chunk // 128) + p]
            if to_far:
                first.append(to_core(given.at[y1, y2], taken.at[y1, y2], yy))
                first[-1].start()

    total = jnp.sum(sq[...]) + jnp.sum(delta_b * delta_b)
    own_factor[...] = jnp.minimum(1.0, bound / jnp.sqrt(jnp.broadcast_to(total, (8, 128)) + epsilon))
    first.append(to_core(own_factor, far_factor, SIDE))
    first[-1].start()
    for d in first:
        d.wait_recv()
    slab = sum_slabs(kept, taken, own_factor[...], far_factor[...], chains, ssend, srecv)
    val = jnp.where(z % 2 == 1, slab[:, ROWS_A:], slab[:, :ROWS_A])
    oa_ref[...] = val[:ROWS_A].T + bound * na_ref[...]
    ob_ref[...] = val[ROWS_A:] + bound * nb_ref[...]
    for d in first:
        d.wait_send()

    for k in range(steps + 1):
        s, _, p, _ = bufs(k)
        most = s.at[: slots - ROWS_F]
        pltpu.make_async_copy(most, most, fsend.at[k]).wait()
        most = p.at[: slots - ROWS_G]
        pltpu.make_async_copy(most, most, gsend.at[k]).wait()
    for h in range(PARTS):
        sent = wf.at[0, :15, h * PIECE : (h + 1) * PIECE]
        pltpu.make_async_copy(sent, sent, wsend.at[h]).wait()
        pltpu.make_async_copy(sent, sent, csend.at[h]).wait()


def main(caps, count, bound, user, tokens, goals, weight, at, b, noise_a, noise_b):
    width, kv = tokens.shape[1], b.shape[1]
    slots = ROWS_F * SIDE * SIDE
    chunk = 1024
    steps = width // chunk
    extra = kv + 128
    whole = pl.BlockSpec(memory_space=pltpu.VMEM)
    scalars = pl.BlockSpec(memory_space=pltpu.SMEM)
    four = [pltpu.VMEM((slots, extra), BF16), pltpu.VMEM((steps, slots, chunk), BF16)] * 4
    dma = pltpu.SemaphoreType.DMA

    slabs = pltpu.VMEM((2, 2, 2, 2, 2, SLAB, 128), F32)

    def chain(route):
        left, bufs = 5, []
        for dim in ("start", *route):
            if dim in ("y1", "y2", "x1", "x2", "z"):
                left -= 1
            lead = (SIDE - 1,) if dim == "ring" else (2,) * left
            bufs.append(pltpu.VMEM((*lead, THIRD, 128), F32))
        return tuple(bufs)

    return pl.pallas_call(
        main_kernel,
        out_shape=tuple(jax.ShapeDtypeStruct(n.shape, F32) for n in (noise_a, noise_b)),
        in_specs=[scalars] * 3 + [whole] * 3 + [pl.BlockSpec(memory_space=pl.ANY)] + [whole] * 4,
        out_specs=(whole, whole),
        scratch_shapes=[
            pltpu.VMEM((slots, tokens.shape[0]), BF16),
            *four,
            pltpu.VMEM((2, SIDE * SIDE, weight.shape[0], kv // 2), BF16),
            pltpu.VMEM((2, slots, kv // 2), F32),
            pltpu.VMEM((slots, at.shape[0]), F32),
            pltpu.VMEM((at.shape[0], width), F32),
            pltpu.VMEM(b.shape, F32),
            pltpu.VMEM((at.shape[0], 128), F32),
            slabs,
            slabs,
            slabs,
            pltpu.VMEM((width // 128, 8, 128), F32),
            pltpu.VMEM((8, 128), F32),
            pltpu.VMEM((8, 128), F32),
            tuple(chain(r) for r in ROUTES),
            dma((steps + 1,)),
            dma((steps + 1,)),
            dma((steps + 1,)),
            dma((steps + 1,)),
            dma((PARTS,)),
            dma((PARTS, 16)),
            dma((PARTS,)),
            dma((PARTS, 16)),
            dma((2 * PARTS,)),
            dma((SUM_SEMS,)),
            dma((SUM_SEMS,)),
        ],
        compiler_params=pltpu.CompilerParams(
            collective_id=0, has_side_effects=True, vmem_limit_bytes=62 << 20
        ),
        name="exchange_and_adapt",
    )(caps, count, bound, user, tokens, goals, weight, at, b, noise_a, noise_b)


def body(
    tokens,
    targets,
    row_owner_user,
    device_row_count,
    user_row_cap,
    value_weight,
    adapter_down,
    adapter_up,
    clip_norm_bound,
    down_noise,
    up_noise,
):
    update_a, update_b = main(
        user_row_cap, device_row_count, clip_norm_bound, row_owner_user.T, tokens, targets, value_weight,
        adapter_down.T, adapter_up, down_noise, up_noise.T,
    )
    return update_a, update_b.T


def solution(mesh):
    in_specs = (
        P(BOTH, None),
        P(BOTH, None),
        P(BOTH, None),
        P(BOTH),
        P(),
        P("fsdp", None),
        P(),
        P(),
        P(),
        P(BOTH, None),
        P(None, BOTH),
    )
    out_specs = (P(BOTH, None), P(None, BOTH))
    return jax.shard_map(
        body, mesh=mesh, in_specs=in_specs, out_specs=out_specs, check_vma=False
    )
```

```python
import functools

import jax
import jax.numpy as jnp
from jax import lax
from jax.experimental import pallas as pl
from jax.experimental.pallas import tpu as pltpu
from jax.sharding import PartitionSpec as P

STEPS = 2
BOTH = ("grp", "fsdp")
MESH = pl.DeviceIdType.MESH
scale = 2.0
rate = 0.05
epsilon = 1e-06
F32 = jnp.float32
BF16 = jnp.bfloat16
SIDE = 4
ROWS_A = 64
SLAB = 72


def mm(a, b, ca, cb):
    return lax.dot_general(a, b, (((ca,), (cb,)), ((), ())), preferred_element_type=F32)


def places():
    g, f = lax.axis_index("grp"), lax.axis_index("fsdp")
    return g // 2, g % 2, f // SIDE, f % SIDE


def low(i):
    return i + 1 - 2 * (i % 2)


def mirror(i):
    return 3 - i


def bits(i, c):
    u = i // 2
    v = (i + i // 2) % 2
    return c * u + (1 - c) * v, c * v + (1 - c) * u


def sides(i, c):
    return c * mirror(i) + (1 - c) * low(i), c * low(i) + (1 - c) * mirror(i)


ROUTES = [
    ("y1", "y2", "x1", "x2", "ring"),
    ("x1", "x2", "y1", "y2", "ring"),
    ("z", "y1", "y2", "x1", "x2", "pair"),
]
THIRD = SLAB // len(ROUTES)
FIRST_SEM = SIDE + 1
SUM_SEMS = FIRST_SEM + sum(len(r) + 2 * ("ring" in r) for r in ROUTES)


def sum_slabs(kept, taken, factor, far, chains, send, recv):
    y, c, x, z = places()

    def dev(y=y, c=c, x=x, z=z):
        return (y * 2 + c, x * SIDE + z)

    yb, xb, yn, xn = bits(y, c), bits(x, c), sides(y, c), sides(x, c)
    bit = {"y1": yb[0], "y2": yb[1], "x1": xb[0], "x2": xb[1], "z": z // 2}
    to = {
        "y1": dev(y=yn[0]),
        "y2": dev(y=yn[1]),
        "x1": dev(x=xn[0]),
        "x2": dev(x=xn[1]),
        "z": dev(z=mirror(z)),
        "pair": dev(z=low(z)),
    }
    started = []

    def go(src, dst, device):
        n = FIRST_SEM + len(started)
        d = pltpu.make_async_remote_copy(
            src_ref=src, dst_ref=dst, send_sem=send.at[n], recv_sem=recv.at[n],
            device_id=device, device_id_type=MESH,
        )
        d.start()
        started.append(d)
        return d

    near = jnp.concatenate([factor] * (THIRD // 8), axis=0)
    away = jnp.concatenate([far] * (THIRD // 8), axis=0)
    now, dims, flying = [], [], []

    def at(ref, left, dim, i):
        return ref.at[(slice(None),) * left.index(dim) + (i,)]

    def launch(n, step):
        route, bufs = ROUTES[n], chains[n]
        dim, ref, left = route[step], now[n], dims[n]
        into = bufs[step + 1]
        if dim == "ring":
            flying[n] = [
                go(ref.at[(z + j) % SIDE // 2], into.at[j - 1], dev(z=(z + j) % SIDE)) for j in range(1, SIDE)
            ]
        elif dim == "pair":
            flying[n] = [go(ref, into, to[dim])]
        else:
            flying[n] = [go(at(ref, left, dim, 1 - bit[dim]), into, to[dim])]

    def land(n, step):
        route, bufs = ROUTES[n], chains[n]
        dim, ref, left = route[step], now[n], dims[n]
        into = bufs[step + 1]
        for d in flying[n]:
            d.wait_recv()
        if dim == "ring":
            return ref[z // 2] + into[0] + into[1] + into[2]
        if dim == "pair":
            return ref[...] + into[...]
        into[...] += at(ref, left, dim, bit[dim])[...]
        now[n] = into
        dims[n] = [v for v in left if v != dim]
        return None

    results = [None] * len(ROUTES)
    for n in range(len(ROUTES)):
        rows = slice(n * THIRD, (n + 1) * THIRD)
        ref = chains[n][0]
        ref[...] = near * kept[:, :, :, :, :, rows] + away * taken[:, :, :, :, :, rows]
        now.append(ref)
        dims.append(["y1", "y2", "x1", "x2", "z"])
        flying.append(None)
        launch(n, 0)
    for step in range(max(len(r) for r in ROUTES)):
        for n, route in enumerate(ROUTES):
            if step < len(route):
                results[n] = land(n, step)
                if step + 1 < len(route):
                    launch(n, step + 1)
    for d in started:
        d.wait_send()
    return jnp.concatenate(results, axis=0)


ROWS_F = 16
ROWS_G = 32
AHEAD = 2
PARTS = ((0, 176), (176, 384))
PLANES = 384
QUARTER = 32
ORDER = [(1, 0), (0, 1), (3, 0), (0, 3), (1, 1), (3, 3), (1, 3), (3, 1), (2, 0), (0, 2), (2, 1), (1, 2), (2, 3), (3, 2), (2, 2)]


def flip(i, by_low, by_mirror):
    i = i + by_low * (1 - 2 * (i % 2))
    return i + by_mirror * (3 - 2 * i)


def piece(i, h, a, b):
    i0, i1, i2, i3 = i % 2, i // 2 % 2, i // 4 % 2, i // 8
    if h == 1:
        i0, i1, i2, i3 = i1, i0, i3, i2
    return flip(a, i0, i1), flip(b, i2, i3)


def main_kernel(
    cap_ref, count_ref, bound_ref, user_ref, tok_ref, tgt_ref, w_ref, at_ref, b_ref, na_ref, nb_ref,
    oa_ref, ob_ref, place_ref, st, sx, rt, rx, pt, px, gt, gx, wf, acc, hid, a1, bcur, sq,
    given, kept, taken, packed, own_factor, far_factor, chains, fsend, frecv, gsend, grecv, wsend, wrecv, ysend, yrecv, csend, crecv, local, ssend, srecv,
):
    y, c, x, z = places()
    g, f = y * 2 + c, x * SIDE + z
    a, b = (1 - c) * x + c * z, (1 - c) * z + c * x
    width = tok_ref.shape[1]
    kv = b_ref.shape[1]
    chunk = sx.shape[2]
    steps = width // chunk
    slots = st.shape[0]
    half = kv // 2

    def column(pos, core):
        return pos[0] * (SIDE - 3 * core) + pos[1] * (1 + 3 * core)

    f_peers = []
    for dx, dz in ORDER:
        f_peers.append((x + dx) % SIDE * SIDE + (z + dz) % SIDE)
    g_peers = []
    for dy, dc in [(1, 0), (3, 1), (3, 0), (1, 1), (2, 0), (2, 1), (0, 1)]:
        g_peers.append((y + dy) % SIDE * 2 + (c + dc) % 2)

    barrier = pltpu.get_barrier_semaphore()
    for to in f_peers:
        pl.semaphore_signal(barrier, inc=1, device_id=(g, to), device_id_type=MESH)
    for to in g_peers:
        pl.semaphore_signal(barrier, inc=1, device_id=(to, f), device_id_type=MESH)

    keep = []
    for n in range(2):
        keep.append(pltpu.make_async_copy(w_ref.at[:, n * half : (n + 1) * half], wf.at[n, f], local.at[n]))
        keep[-1].start()

    user = user_ref[...]
    per = user.shape[1]
    u_i = lax.broadcasted_iota(jnp.int32, (per, per), 0)
    v_i = lax.broadcasted_iota(jnp.int32, (per, per), 1)
    named = jnp.where(lax.broadcasted_iota(jnp.int32, (128, per), 0) == user, 1.0, 0.0)
    above = jnp.where(u_i < v_i, 1.0, 0.0).astype(BF16)
    rank = jnp.sum(mm(named.astype(BF16), above, 1, 0) * named, axis=0, keepdims=True).astype(jnp.int32)
    slot = (user & 15) * ROWS_F + (user >> 4) * 2 + rank
    place_ref[...] = jnp.where(lax.broadcasted_iota(jnp.int32, (slots, per), 0) == slot, 1.0, 0.0).astype(BF16)
    count = count_ref[0]
    flags = jnp.where(lax.broadcasted_iota(jnp.int32, (per, 128), 0) < count, 1.0, 0.0).astype(BF16)
    place = place_ref[...]
    n_i = lax.broadcasted_iota(jnp.int32, (slots, slots), 0)
    o_i = lax.broadcasted_iota(jnp.int32, (slots, slots), 1)
    old = ((n_i >> 1) & 15) * 16 + (n_i >> 5) * 2 + (n_i & 1)
    turn = jnp.where(o_i == old, 1.0, 0.0).astype(BF16)

    def bufs(k):
        if k == 0:
            return st, rt, pt, gt
        return sx.at[k - 1], rx.at[k - 1], px.at[k - 1], gx.at[k - 1]

    def rows_f(i):
        return pl.ds(pl.multiple_of(i * ROWS_F, ROWS_F), ROWS_F)

    def rows_g(i):
        return pl.ds(pl.multiple_of(i * ROWS_G, ROWS_G), ROWS_G)

    def place_rows(k):
        s = bufs(k)[0]
        if k == 0:
            s[:, :kv] = mm(place, tgt_ref[...], 1, 0).astype(BF16)
            s[:, kv:] = mm(place, flags, 1, 0).astype(BF16)
        else:
            s[...] = mm(place, tok_ref[:, (k - 1) * chunk : k * chunk], 1, 0).astype(BF16)

    def start_f(k):
        s, r, _, _ = bufs(k)
        for to in f_peers:
            pltpu.make_async_remote_copy(
                src_ref=s.at[rows_f(to)], dst_ref=r.at[rows_f(f)], send_sem=fsend.at[k], recv_sem=frecv.at[k],
                device_id=(g, to), device_id_type=MESH,
            ).start()
        r[rows_f(f), :] = s[rows_f(f), :]

    def turn_rows(k):
        _, r, p, q = bufs(k)
        most = r.at[: slots - ROWS_F]
        pltpu.make_async_copy(most, most, frecv.at[k]).wait()
        p[...] = mm(turn, r[...], 1, 0).astype(BF16)
        for to in g_peers:
            pltpu.make_async_remote_copy(
                src_ref=p.at[rows_g(to)], dst_ref=q.at[rows_g(g)], send_sem=gsend.at[k], recv_sem=grecv.at[k],
                device_id=(to, f), device_id_type=MESH,
            ).start()
        q[rows_g(g), :] = p[rows_g(g), :]

    def end_g(k):
        q = bufs(k)[3]
        most = q.at[: slots - ROWS_G]
        pltpu.make_async_copy(most, most, grecv.at[k]).wait()

    def send(src, dst, ssem, rsem, device):
        pltpu.make_async_remote_copy(
            src_ref=src, dst_ref=dst, send_sem=ssem, recv_sem=rsem, device_id=device, device_id_type=MESH
        ).start()

    def await_bytes(ref, sem):
        pltpu.make_async_copy(ref, ref, sem).wait()

    yn = sides(y, c)
    beyond = sides(yn[1], c)[0]
    my_half = pl.ds(pl.multiple_of(c * half, half), half)

    def quarter(q):
        return pl.ds(pl.multiple_of(PLANES + q * QUARTER, 16), QUARTER)

    def col_of(i, h=0):
        return column(piece(i, h, a, b), c)

    def pass_on(i, h):
        rows = slice(*PARTS[h])
        ref = wf.at[c, col_of(i, h), rows]
        src = ref
        if i == 0:
            src = w_ref.at[rows, my_half]
        else:
            await_bytes(ref, wrecv.at[h, i])
        for n in range(i.bit_length(), 4):
            send(src, ref, wsend.at[h], wrecv.at[h, (1 << n) + i], (g, col_of(1 << n, h)))

    def pass_quarter(i, level):
        ref = wf.at[c, col_of(i), quarter(y)]
        src = ref
        if level == 0:
            src = w_ref.at[quarter(y), my_half]
        else:
            await_bytes(ref, yrecv.at[0, i])
        for n in range(level, 4):
            send(src, ref, ysend.at[0], yrecv.at[0, (1 << n) + i], (g, col_of(1 << n)))
        if level:
            for n in range(2):
                send(ref, ref, ysend.at[1 + n], yrecv.at[1 + n, i], (yn[n] * 2 + c, f))

    def relay(i):
        ref = wf.at[c, col_of(i), quarter(yn[0])]
        await_bytes(ref, yrecv.at[1, i])
        send(ref, ref, ysend.at[3], yrecv.at[3, i], (yn[1] * 2 + c, f))

    def add(n, col):
        depth = w_ref.shape[0]
        per = chunk // depth
        x_cols = gx[col // per, :, pl.ds(pl.multiple_of(col % per * depth, depth), depth)]
        acc[n] += mm(x_cols, wf[n, col], 1, 0)

    def add_other(i):
        col = column(piece(i, 0, b, a), 1 - c)
        await_bytes(wf.at[1 - c, col], crecv.at[i])
        add(1 - c, col)

    place_rows(0)
    pl.semaphore_wait(barrier, len(f_peers) + len(g_peers))
    start_f(0)
    place_rows(1)
    start_f(1)
    acc[...] = jnp.zeros_like(acc)
    hid[...] = jnp.zeros_like(hid)
    both = range(len(PARTS))
    def last_quarters():
        @pl.loop(8, 16)
        def _(i):
            pass_quarter(i, 4)

    def relays(lo, hi):
        @pl.loop(lo, hi)
        def _(i):
            relay(i)

    todo = {
        1: lambda: pass_quarter(0, 0),
        2: lambda: pass_quarter(1, 1),
        3: lambda: [pass_quarter(i, 2) for i in (2, 3)],
        4: lambda: [pass_quarter(i, 3) for i in (4, 5, 6, 7)],
        5: lambda: [pass_on(0, h) for h in both] + [last_quarters()],
        7: lambda: [pass_on(1, h) for h in both] + [relays(1, 8)],
        8: lambda: [relays(8, 16)],
        9: lambda: [pass_on(i, h) for i in (2, 3) for h in both],
        10: lambda: [pass_on(i, h) for i in (4, 5, 6, 7) for h in both],
    }
    for k in range(1, steps + 1 + AHEAD):
        if 1 < k <= steps:
            place_rows(k)
            start_f(k)
        if k >= AHEAD:
            turn_rows(k - AHEAD)
        if k in todo:
            todo[k]()

    end_g(0)
    for k in range(1, steps + 1):
        end_g(k)
        hid[...] += mm(gx[k - 1], at_ref[:, (k - 1) * chunk : k * chunk], 1, 1)
    for d in keep:
        d.wait()
    for n in range(2):
        add(n, f)

    @pl.loop(1, 16)
    def _(i):
        col = col_of(i)
        twin = i % 2 * 2 + i // 2 % 2 + i // 4 % 2 * 8 + i // 8 * 4

        @pl.when(i >= 8)
        def _():
            await_bytes(wf.at[c, col, slice(*PARTS[0])], wrecv.at[0, i])

        @pl.when(twin >= 8)
        def _():
            await_bytes(wf.at[c, col, slice(*PARTS[1])], wrecv.at[1, twin])

        await_bytes(wf.at[c, col, quarter(yn[1])], yrecv.at[2, i])
        await_bytes(wf.at[c, col, quarter(beyond)], yrecv.at[3, i])
        shard = wf.at[c, col]
        send(shard, shard, csend.at[0], crecv.at[i], (y * 2 + 1 - c, f))
        add(c, col)

        @pl.when(i >= 3)
        def _():
            add_other(i - 2)

    add_other(14)
    add_other(15)

    cap, bound = cap_ref[g * SIDE * SIDE + f].astype(F32), bound_ref[0]
    used = gt[:, kv:]
    before = jnp.where(o_i < n_i, 1.0, 0.0).astype(BF16)
    earlier = mm(before, used, 1, 0)
    live = jnp.where((used.astype(F32) > 0.5) & (earlier < cap), 1.0 / cap, 0.0)
    live = jnp.concatenate([live] * (kv // live.shape[1]), axis=1)
    base = jnp.concatenate([acc[0], acc[1]], axis=1) - gt[:, :kv].astype(F32)

    def part(k):
        return pl.ds(pl.multiple_of(k * chunk, chunk), chunk)

    def errors(h, b16):
        r = (live * (base + scale * mm(h, b16, 1, 0))).astype(BF16)
        return mm(r, b16, 1, 1).astype(BF16), scale * mm(h, r, 0, 0)

    b0 = b_ref[...]
    back, grad_b = errors(hid[...].astype(BF16), b0)
    bcur[...] = b0.astype(F32) - rate * grad_b
    hid[...] = jnp.zeros_like(hid)

    @pl.loop(0, steps)
    def _(k):
        rows = gx[k]
        now = at_ref[:, part(k)].astype(F32) - rate * (scale * mm(back, rows, 0, 0))
        a1[:, part(k)] = now
        hid[...] += mm(rows, now.astype(BF16), 1, 1)

    back2, grad_b2 = errors(hid[...].astype(BF16), bcur[...].astype(BF16))
    delta_b = (bcur[...] - rate * grad_b2) - b0.astype(F32)
    sq[...] = jnp.zeros_like(sq)

    bt = delta_b.T.reshape(width // 128, 16, ROWS_A)
    packed[...] = jnp.concatenate([bt[:, :8, :], bt[:, 8:, :]], axis=2)
    other_core = (y * 2 + 1 - c, f)

    def to_core(src, dst, n):
        return pltpu.make_async_remote_copy(
            src_ref=src, dst_ref=dst, send_sem=ssend.at[n], recv_sem=srecv.at[n],
            device_id=other_core, device_id_type=MESH,
        )

    first = []
    for to_far in (True, False):
        core = 1 - c if to_far else c
        slabs = given if to_far else kept
        for yy in range(SIDE):
            k = yy * 2 + core
            d = (a1[:, part(k)] - rate * (scale * mm(back2, gx[k], 0, 0))) - at_ref[:, part(k)].astype(F32)
            sq[...] += jnp.sum((d * d).reshape(d.shape[0], chunk // 128, 128), axis=1)
            y1, y2 = bits(yy, core)
            for p in range(chunk // 128):
                x1, x2 = bits(p // 2, core)
                slabs[y1, y2, x1, x2, p % 2, :ROWS_A, :] = d[:, p * 128 : (p + 1) * 128]
                slabs[y1, y2, x1, x2, p % 2, ROWS_A:, :] = packed[k * (chunk // 128) + p]
            if to_far:
                first.append(to_core(given.at[y1, y2], taken.at[y1, y2], yy))
                first[-1].start()

    total = jnp.sum(sq[...]) + jnp.sum(delta_b * delta_b)
    own_factor[...] = jnp.minimum(1.0, bound / jnp.sqrt(jnp.broadcast_to(total, (8, 128)) + epsilon))
    first.append(to_core(own_factor, far_factor, SIDE))
    first[-1].start()
    for d in first:
        d.wait_recv()
    slab = sum_slabs(kept, taken, own_factor[...], far_factor[...], chains, ssend, srecv)
    val = jnp.where(z % 2 == 1, slab[:, ROWS_A:], slab[:, :ROWS_A])
    oa_ref[...] = val[:ROWS_A].T + bound * na_ref[...]
    ob_ref[...] = val[ROWS_A:] + bound * nb_ref[...]
    for d in first:
        d.wait_send()

    for k in range(steps + 1):
        s, _, p, _ = bufs(k)
        most = s.at[: slots - ROWS_F]
        pltpu.make_async_copy(most, most, fsend.at[k]).wait()
        most = p.at[: slots - ROWS_G]
        pltpu.make_async_copy(most, most, gsend.at[k]).wait()
    for h in both:
        await_bytes(wf.at[0, :15, slice(*PARTS[h])], wsend.at[h])
    for n in range(4):
        await_bytes(wf.at[0, :15, :QUARTER], ysend.at[n])
    await_bytes(wf.at[0, :15], csend.at[0])


def main(caps, count, bound, user, tokens, goals, weight, at, b, noise_a, noise_b):
    width, kv = tokens.shape[1], b.shape[1]
    slots = ROWS_F * SIDE * SIDE
    chunk = 1024
    steps = width // chunk
    extra = kv + 128
    whole = pl.BlockSpec(memory_space=pltpu.VMEM)
    scalars = pl.BlockSpec(memory_space=pltpu.SMEM)
    four = [pltpu.VMEM((slots, extra), BF16), pltpu.VMEM((steps, slots, chunk), BF16)] * 4
    dma = pltpu.SemaphoreType.DMA

    slabs = pltpu.VMEM((2, 2, 2, 2, 2, SLAB, 128), F32)

    def chain(route):
        left, bufs = 5, []
        for dim in ("start", *route):
            if dim in ("y1", "y2", "x1", "x2", "z"):
                left -= 1
            lead = (SIDE - 1,) if dim == "ring" else (2,) * left
            bufs.append(pltpu.VMEM((*lead, THIRD, 128), F32))
        return tuple(bufs)

    return pl.pallas_call(
        main_kernel,
        out_shape=tuple(jax.ShapeDtypeStruct(n.shape, F32) for n in (noise_a, noise_b)),
        in_specs=[scalars] * 3 + [whole] * 3 + [pl.BlockSpec(memory_space=pl.ANY)] + [whole] * 4,
        out_specs=(whole, whole),
        scratch_shapes=[
            pltpu.VMEM((slots, tokens.shape[0]), BF16),
            *four,
            pltpu.VMEM((2, SIDE * SIDE, weight.shape[0], kv // 2), BF16),
            pltpu.VMEM((2, slots, kv // 2), F32),
            pltpu.VMEM((slots, at.shape[0]), F32),
            pltpu.VMEM((at.shape[0], width), F32),
            pltpu.VMEM(b.shape, F32),
            pltpu.VMEM((at.shape[0], 128), F32),
            slabs,
            slabs,
            slabs,
            pltpu.VMEM((width // 128, 8, 128), F32),
            pltpu.VMEM((8, 128), F32),
            pltpu.VMEM((8, 128), F32),
            tuple(chain(r) for r in ROUTES),
            dma((steps + 1,)),
            dma((steps + 1,)),
            dma((steps + 1,)),
            dma((steps + 1,)),
            dma((len(PARTS),)),
            dma((len(PARTS), 16)),
            dma((4,)),
            dma((4, 16)),
            dma((1,)),
            dma((16,)),
            dma((2,)),
            dma((SUM_SEMS,)),
            dma((SUM_SEMS,)),
        ],
        compiler_params=pltpu.CompilerParams(
            collective_id=0, has_side_effects=True, vmem_limit_bytes=62 << 20
        ),
        name="exchange_and_adapt",
    )(caps, count, bound, user, tokens, goals, weight, at, b, noise_a, noise_b)


def body(
    tokens,
    targets,
    row_owner_user,
    device_row_count,
    user_row_cap,
    value_weight,
    adapter_down,
    adapter_up,
    clip_norm_bound,
    down_noise,
    up_noise,
):
    update_a, update_b = main(
        user_row_cap, device_row_count, clip_norm_bound, row_owner_user.T, tokens, targets, value_weight,
        adapter_down.T, adapter_up, down_noise, up_noise.T,
    )
    return update_a, update_b.T


def solution(mesh):
    in_specs = (
        P(BOTH, None),
        P(BOTH, None),
        P(BOTH, None),
        P(BOTH),
        P(),
        P("fsdp", None),
        P(),
        P(),
        P(),
        P(BOTH, None),
        P(None, BOTH),
    )
    out_specs = (P(BOTH, None), P(None, BOTH))
    return jax.shard_map(
        body, mesh=mesh, in_specs=in_specs, out_specs=out_specs, check_vma=False
    )
```

```python
import functools

import jax
import jax.numpy as jnp
from jax import lax
from jax.experimental import pallas as pl
from jax.experimental.pallas import tpu as pltpu
from jax.sharding import PartitionSpec as P

STEPS = 2
BOTH = ("grp", "fsdp")
MESH = pl.DeviceIdType.MESH
scale = 2.0
rate = 0.05
epsilon = 1e-06
F32 = jnp.float32
BF16 = jnp.bfloat16
SIDE = 4
ROWS_A = 64
SLAB = 72


def mm(a, b, ca, cb):
    return lax.dot_general(a, b, (((ca,), (cb,)), ((), ())), preferred_element_type=F32)


def places():
    g, f = lax.axis_index("grp"), lax.axis_index("fsdp")
    return g // 2, g % 2, f // SIDE, f % SIDE


def low(i):
    return i + 1 - 2 * (i % 2)


def mirror(i):
    return 3 - i


def bits(i, c):
    u = i // 2
    v = (i + i // 2) % 2
    return c * u + (1 - c) * v, c * v + (1 - c) * u


def sides(i, c):
    return c * mirror(i) + (1 - c) * low(i), c * low(i) + (1 - c) * mirror(i)


ROUTES = [
    ("y1", "y2", "xz"),
    ("x1", "x2", "yz"),
    ("z", "y1", "block"),
]
LAST = {
    "xz": [(0, dx, dz) for dx in range(SIDE) for dz in range(SIDE)][1:],
    "yz": [(dy, 0, dz) for dy in range(SIDE) for dz in range(SIDE)][1:],
    "block": [(n, dx, m) for n in ("same", "second") for dx in range(SIDE) for m in ("same", "low")][1:],
}
THIRD = SLAB // len(ROUTES)
FIRST_SEM = SIDE + 1
SUM_SEMS = FIRST_SEM + sum(len(LAST.get(dim, (0,))) for r in ROUTES for dim in r)


def sum_slabs(kept, taken, factor, far, chains, send, recv):
    y, c, x, z = places()

    def dev(y=y, x=x, z=z):
        return (y * 2 + c, x * SIDE + z)

    yb, xb, yn, xn = bits(y, c), bits(x, c), sides(y, c), sides(x, c)
    bit = {"y1": yb[0], "y2": yb[1], "x1": xb[0], "x2": xb[1], "z": z // 2}
    to = {
        "y1": dev(y=yn[0]),
        "y2": dev(y=yn[1]),
        "x1": dev(x=xn[0]),
        "x2": dev(x=xn[1]),
        "z": dev(z=mirror(z)),
    }
    started = []

    def go(src, dst, device):
        n = FIRST_SEM + len(started)
        d = pltpu.make_async_remote_copy(
            src_ref=src, dst_ref=dst, send_sem=send.at[n], recv_sem=recv.at[n],
            device_id=device, device_id_type=MESH,
        )
        d.start()
        started.append(d)
        return d

    near = jnp.concatenate([factor] * (THIRD // 8), axis=0)
    away = jnp.concatenate([far] * (THIRD // 8), axis=0)
    now, dims, flying = [], [], []

    def at(ref, left, dim, i):
        return ref.at[(slice(None),) * left.index(dim) + (i,)]

    def slab_of(ref, left, y, x, z):
        own = dict(zip(("y1", "y2", "x1", "x2", "z"), (*bits(y, c), *bits(x, c), z // 2)))
        return ref.at[tuple(own[d] for d in left)]

    def launch(n, step):
        dim, ref, left = ROUTES[n][step], now[n], dims[n]
        into = chains[n][step + 1]
        if dim in LAST:
            flying[n] = []
            for k, (dy, dx, dz) in enumerate(LAST[dim]):
                zz = z if dz == "same" else low(z) if dz == "low" else (z + dz) % SIDE
                yy = y if dy == "same" else yn[1] if dy == "second" else (y + dy) % SIDE
                xx = (x + dx) % SIDE
                flying[n].append(go(slab_of(ref, left, yy, xx, zz), into.at[k], dev(yy, xx, zz)))
        else:
            flying[n] = [go(at(ref, left, dim, 1 - bit[dim]), into, to[dim])]

    def land(n, step):
        dim, ref, left = ROUTES[n][step], now[n], dims[n]
        into = chains[n][step + 1]
        for d in flying[n]:
            d.wait_recv()
        if dim in LAST:
            return slab_of(ref, left, y, x, z)[...] + jnp.sum(into[...], axis=0)
        into[...] += at(ref, left, dim, bit[dim])[...]
        now[n] = into
        dims[n] = [v for v in left if v != dim]
        return None

    results = [None] * len(ROUTES)
    for n in range(len(ROUTES)):
        rows = slice(n * THIRD, (n + 1) * THIRD)
        chains[n][0][...] = near * kept[:, :, :, :, :, rows] + away * taken[:, :, :, :, :, rows]
        now.append(chains[n][0])
        dims.append(["y1", "y2", "x1", "x2", "z"])
        flying.append(None)
        launch(n, 0)
    for step in range(max(len(r) for r in ROUTES)):
        for n, route in enumerate(ROUTES):
            if step < len(route):
                results[n] = land(n, step)
                if step + 1 < len(route):
                    launch(n, step + 1)
    for d in started:
        d.wait_send()
    return jnp.concatenate(results, axis=0)


ROWS_F = 16
ROWS_G = 32
AHEAD = 2
PARTS = ((0, 176), (176, 384))
PLANES = 384
QUARTER = 32
ORDER = [(1, 0), (0, 1), (3, 0), (0, 3), (1, 1), (3, 3), (1, 3), (3, 1), (2, 0), (0, 2), (2, 1), (1, 2), (2, 3), (3, 2), (2, 2)]


def flip(i, by_low, by_mirror):
    i = i + by_low * (1 - 2 * (i % 2))
    return i + by_mirror * (3 - 2 * i)


def piece(i, h, a, b):
    i0, i1, i2, i3 = i % 2, i // 2 % 2, i // 4 % 2, i // 8
    if h == 1:
        i0, i1, i2, i3 = i1, i0, i3, i2
    return flip(a, i0, i1), flip(b, i2, i3)


def main_kernel(
    cap_ref, count_ref, bound_ref, user_ref, tok_ref, tgt_ref, w_ref, at_ref, b_ref,
    oa_ref, ob_ref, place_ref, st, sx, rt, rx, pt, px, gt, gx, wf, acc, hid, a1, bcur, sq,
    given, kept, taken, packed, own_factor, far_factor, chains, fsend, frecv, gsend, grecv, wsend, wrecv, ysend, yrecv, csend, crecv, local, ssend, srecv,
):
    y, c, x, z = places()
    g, f = y * 2 + c, x * SIDE + z
    a, b = (1 - c) * x + c * z, (1 - c) * z + c * x
    width = tok_ref.shape[1]
    kv = b_ref.shape[1]
    chunk = sx.shape[2]
    steps = width // chunk
    slots = st.shape[0]
    half = kv // 2

    def column(pos, core):
        return pos[0] * (SIDE - 3 * core) + pos[1] * (1 + 3 * core)

    f_peers = []
    for dx, dz in ORDER:
        f_peers.append((x + dx) % SIDE * SIDE + (z + dz) % SIDE)
    g_peers = []
    for dy, dc in [(1, 0), (3, 1), (3, 0), (1, 1), (2, 0), (2, 1), (0, 1)]:
        g_peers.append((y + dy) % SIDE * 2 + (c + dc) % 2)

    barrier = pltpu.get_barrier_semaphore()
    for to in f_peers:
        pl.semaphore_signal(barrier, inc=1, device_id=(g, to), device_id_type=MESH)
    for to in g_peers:
        pl.semaphore_signal(barrier, inc=1, device_id=(to, f), device_id_type=MESH)
    further = [((y + dy) % SIDE, x, (z + dz) % SIDE) for dy in range(1, SIDE) for dz in range(1, SIDE)]
    further += [(sides(y, c)[1], (x + dx) % SIDE, zz) for dx in range(1, SIDE) for zz in (z, low(z))]
    for ty, tx, tz in further:
        pl.semaphore_signal(barrier, inc=1, device_id=(ty * 2 + c, tx * SIDE + tz), device_id_type=MESH)

    keep = []
    for n in range(2):
        keep.append(pltpu.make_async_copy(w_ref.at[:, n * half : (n + 1) * half], wf.at[n, f], local.at[n]))
        keep[-1].start()

    user = user_ref[...]
    per = user.shape[1]
    u_i = lax.broadcasted_iota(jnp.int32, (per, per), 0)
    v_i = lax.broadcasted_iota(jnp.int32, (per, per), 1)
    named = jnp.where(lax.broadcasted_iota(jnp.int32, (128, per), 0) == user, 1.0, 0.0)
    above = jnp.where(u_i < v_i, 1.0, 0.0).astype(BF16)
    rank = jnp.sum(mm(named.astype(BF16), above, 1, 0) * named, axis=0, keepdims=True).astype(jnp.int32)
    slot = (user & 15) * ROWS_F + (user >> 4) * 2 + rank
    place_ref[...] = jnp.where(lax.broadcasted_iota(jnp.int32, (slots, per), 0) == slot, 1.0, 0.0).astype(BF16)
    count = count_ref[0]
    flags = jnp.where(lax.broadcasted_iota(jnp.int32, (per, 128), 0) < count, 1.0, 0.0).astype(BF16)
    place = place_ref[...]
    n_i = lax.broadcasted_iota(jnp.int32, (slots, slots), 0)
    o_i = lax.broadcasted_iota(jnp.int32, (slots, slots), 1)
    old = ((n_i >> 1) & 15) * 16 + (n_i >> 5) * 2 + (n_i & 1)
    turn = jnp.where(o_i == old, 1.0, 0.0).astype(BF16)

    def bufs(k):
        if k == 0:
            return st, rt, pt, gt
        return sx.at[k - 1], rx.at[k - 1], px.at[k - 1], gx.at[k - 1]

    def rows_f(i):
        return pl.ds(pl.multiple_of(i * ROWS_F, ROWS_F), ROWS_F)

    def rows_g(i):
        return pl.ds(pl.multiple_of(i * ROWS_G, ROWS_G), ROWS_G)

    def place_rows(k):
        s = bufs(k)[0]
        if k == 0:
            s[:, :kv] = mm(place, tgt_ref[...], 1, 0).astype(BF16)
            s[:, kv:] = mm(place, flags, 1, 0).astype(BF16)
        else:
            s[...] = mm(place, tok_ref[:, (k - 1) * chunk : k * chunk], 1, 0).astype(BF16)

    def start_f(k):
        s, r, _, _ = bufs(k)
        for to in f_peers:
            pltpu.make_async_remote_copy(
                src_ref=s.at[rows_f(to)], dst_ref=r.at[rows_f(f)], send_sem=fsend.at[k], recv_sem=frecv.at[k],
                device_id=(g, to), device_id_type=MESH,
            ).start()
        r[rows_f(f), :] = s[rows_f(f), :]

    def turn_rows(k):
        _, r, p, q = bufs(k)
        most = r.at[: slots - ROWS_F]
        pltpu.make_async_copy(most, most, frecv.at[k]).wait()
        p[...] = mm(turn, r[...], 1, 0).astype(BF16)
        for to in g_peers:
            pltpu.make_async_remote_copy(
                src_ref=p.at[rows_g(to)], dst_ref=q.at[rows_g(g)], send_sem=gsend.at[k], recv_sem=grecv.at[k],
                device_id=(to, f), device_id_type=MESH,
            ).start()
        q[rows_g(g), :] = p[rows_g(g), :]

    def end_g(k):
        q = bufs(k)[3]
        most = q.at[: slots - ROWS_G]
        pltpu.make_async_copy(most, most, grecv.at[k]).wait()

    def send(src, dst, ssem, rsem, device):
        pltpu.make_async_remote_copy(
            src_ref=src, dst_ref=dst, send_sem=ssem, recv_sem=rsem, device_id=device, device_id_type=MESH
        ).start()

    def await_bytes(ref, sem):
        pltpu.make_async_copy(ref, ref, sem).wait()

    yn = sides(y, c)
    beyond = sides(yn[1], c)[0]
    my_half = pl.ds(pl.multiple_of(c * half, half), half)

    def quarter(q):
        return pl.ds(pl.multiple_of(PLANES + q * QUARTER, 16), QUARTER)

    def col_of(i, h=0):
        return column(piece(i, h, a, b), c)

    def pass_on(i, h):
        rows = slice(*PARTS[h])
        ref = wf.at[c, col_of(i, h), rows]
        src = ref
        if i == 0:
            src = w_ref.at[rows, my_half]
        else:
            await_bytes(ref, wrecv.at[h, i])
        for n in range(i.bit_length(), 4):
            send(src, ref, wsend.at[h], wrecv.at[h, (1 << n) + i], (g, col_of(1 << n, h)))

    def pass_quarter(i, level):
        ref = wf.at[c, col_of(i), quarter(y)]
        src = ref
        if level == 0:
            src = w_ref.at[quarter(y), my_half]
        else:
            await_bytes(ref, yrecv.at[0, i])
        for n in range(level, 4):
            send(src, ref, ysend.at[0], yrecv.at[0, (1 << n) + i], (g, col_of(1 << n)))
        if level:
            for n in range(2):
                send(ref, ref, ysend.at[1 + n], yrecv.at[1 + n, i], (yn[n] * 2 + c, f))

    def relay(i):
        ref = wf.at[c, col_of(i), quarter(yn[0])]
        await_bytes(ref, yrecv.at[1, i])
        send(ref, ref, ysend.at[3], yrecv.at[3, i], (yn[1] * 2 + c, f))

    def add(n, col):
        depth = w_ref.shape[0]
        per = chunk // depth
        x_cols = gx[col // per, :, pl.ds(pl.multiple_of(col % per * depth, depth), depth)]
        acc[n] += mm(x_cols, wf[n, col], 1, 0)

    def add_other(i):
        col = column(piece(i, 0, b, a), 1 - c)
        await_bytes(wf.at[1 - c, col], crecv.at[i])
        add(1 - c, col)

    place_rows(0)
    pl.semaphore_wait(barrier, len(f_peers) + len(g_peers) + len(further))
    start_f(0)
    place_rows(1)
    start_f(1)
    acc[...] = jnp.zeros_like(acc)
    hid[...] = jnp.zeros_like(hid)
    both = range(len(PARTS))
    def last_quarters():
        @pl.loop(8, 16)
        def _(i):
            pass_quarter(i, 4)

    def relays(lo, hi):
        @pl.loop(lo, hi)
        def _(i):
            relay(i)

    todo = {
        1: lambda: pass_quarter(0, 0),
        2: lambda: pass_quarter(1, 1),
        3: lambda: [pass_quarter(i, 2) for i in (2, 3)],
        4: lambda: [pass_quarter(i, 3) for i in (4, 5, 6, 7)],
        5: lambda: [pass_on(0, h) for h in both] + [last_quarters()],
        7: lambda: [pass_on(1, h) for h in both] + [relays(1, 8)],
        8: lambda: [relays(8, 16)],
        9: lambda: [pass_on(i, h) for i in (2, 3) for h in both],
        10: lambda: [pass_on(i, h) for i in (4, 5, 6, 7) for h in both],
    }
    for k in range(1, steps + 1 + AHEAD):
        if 1 < k <= steps:
            place_rows(k)
            start_f(k)
        if k >= AHEAD:
            turn_rows(k - AHEAD)
        if k in todo:
            todo[k]()

    end_g(0)
    for k in range(1, steps + 1):
        end_g(k)
        hid[...] += mm(gx[k - 1], at_ref[:, (k - 1) * chunk : k * chunk], 1, 1)
    for d in keep:
        d.wait()
    for n in range(2):
        add(n, f)

    @pl.loop(1, 16)
    def _(i):
        col = col_of(i)
        twin = i % 2 * 2 + i // 2 % 2 + i // 4 % 2 * 8 + i // 8 * 4

        @pl.when(i >= 8)
        def _():
            await_bytes(wf.at[c, col, slice(*PARTS[0])], wrecv.at[0, i])

        @pl.when(twin >= 8)
        def _():
            await_bytes(wf.at[c, col, slice(*PARTS[1])], wrecv.at[1, twin])

        await_bytes(wf.at[c, col, quarter(yn[1])], yrecv.at[2, i])
        await_bytes(wf.at[c, col, quarter(beyond)], yrecv.at[3, i])
        shard = wf.at[c, col]
        send(shard, shard, csend.at[0], crecv.at[i], (y * 2 + 1 - c, f))
        add(c, col)

        @pl.when(i >= 3)
        def _():
            add_other(i - 2)

    add_other(14)
    add_other(15)

    cap, bound = cap_ref[g * SIDE * SIDE + f].astype(F32), bound_ref[0]
    used = gt[:, kv:]
    before = jnp.where(o_i < n_i, 1.0, 0.0).astype(BF16)
    earlier = mm(before, used, 1, 0)
    live = jnp.where((used.astype(F32) > 0.5) & (earlier < cap), 1.0 / cap, 0.0)
    live = jnp.concatenate([live] * (kv // live.shape[1]), axis=1)
    base = jnp.concatenate([acc[0], acc[1]], axis=1) - gt[:, :kv].astype(F32)

    def part(k):
        return pl.ds(pl.multiple_of(k * chunk, chunk), chunk)

    def errors(h, b16):
        r = (live * (base + scale * mm(h, b16, 1, 0))).astype(BF16)
        return mm(r, b16, 1, 1).astype(BF16), scale * mm(h, r, 0, 0)

    b0 = b_ref[...]
    back, grad_b = errors(hid[...].astype(BF16), b0)
    bcur[...] = b0.astype(F32) - rate * grad_b
    hid[...] = jnp.zeros_like(hid)

    @pl.loop(0, steps)
    def _(k):
        rows = gx[k]
        now = at_ref[:, part(k)].astype(F32) - rate * (scale * mm(back, rows, 0, 0))
        a1[:, part(k)] = now
        hid[...] += mm(rows, now.astype(BF16), 1, 1)

    back2, grad_b2 = errors(hid[...].astype(BF16), bcur[...].astype(BF16))
    delta_b = (bcur[...] - rate * grad_b2) - b0.astype(F32)
    sq[...] = jnp.zeros_like(sq)

    bt = delta_b.T.reshape(width // 128, 16, ROWS_A)
    packed[...] = jnp.concatenate([bt[:, :8, :], bt[:, 8:, :]], axis=2)
    other_core = (y * 2 + 1 - c, f)

    def to_core(src, dst, n):
        return pltpu.make_async_remote_copy(
            src_ref=src, dst_ref=dst, send_sem=ssend.at[n], recv_sem=srecv.at[n],
            device_id=other_core, device_id_type=MESH,
        )

    first = []
    for to_far in (True, False):
        core = 1 - c if to_far else c
        slabs = given if to_far else kept
        for yy in range(SIDE):
            k = yy * 2 + core
            d = (a1[:, part(k)] - rate * (scale * mm(back2, gx[k], 0, 0))) - at_ref[:, part(k)].astype(F32)
            sq[...] += jnp.sum((d * d).reshape(d.shape[0], chunk // 128, 128), axis=1)
            y1, y2 = bits(yy, core)
            for p in range(chunk // 128):
                x1, x2 = bits(p // 2, core)
                slabs[y1, y2, x1, x2, p % 2, :ROWS_A, :] = d[:, p * 128 : (p + 1) * 128]
                slabs[y1, y2, x1, x2, p % 2, ROWS_A:, :] = packed[k * (chunk // 128) + p]
            if to_far:
                first.append(to_core(given.at[y1, y2], taken.at[y1, y2], yy))
                first[-1].start()

    total = jnp.sum(sq[...]) + jnp.sum(delta_b * delta_b)
    own_factor[...] = jnp.minimum(1.0, bound / jnp.sqrt(jnp.broadcast_to(total, (8, 128)) + epsilon))
    first.append(to_core(own_factor, far_factor, SIDE))
    first[-1].start()
    for d in first:
        d.wait_recv()
    slab = sum_slabs(kept, taken, own_factor[...], far_factor[...], chains, ssend, srecv)
    val = jnp.where(z % 2 == 1, slab[:, ROWS_A:], slab[:, :ROWS_A])
    oa_ref[...] = val[:ROWS_A].T
    ob_ref[...] = val[ROWS_A:]
    for d in first:
        d.wait_send()

    for k in range(steps + 1):
        s, _, p, _ = bufs(k)
        most = s.at[: slots - ROWS_F]
        pltpu.make_async_copy(most, most, fsend.at[k]).wait()
        most = p.at[: slots - ROWS_G]
        pltpu.make_async_copy(most, most, gsend.at[k]).wait()
    for h in both:
        await_bytes(wf.at[0, :15, slice(*PARTS[h])], wsend.at[h])
    for n in range(4):
        await_bytes(wf.at[0, :15, :QUARTER], ysend.at[n])
    await_bytes(wf.at[0, :15], csend.at[0])


def main(caps, count, bound, user, tokens, goals, weight, at, b, outs):
    width, kv = tokens.shape[1], b.shape[1]
    slots = ROWS_F * SIDE * SIDE
    chunk = 1024
    steps = width // chunk
    extra = kv + 128
    whole = pl.BlockSpec(memory_space=pltpu.VMEM)
    scalars = pl.BlockSpec(memory_space=pltpu.SMEM)
    four = [pltpu.VMEM((slots, extra), BF16), pltpu.VMEM((steps, slots, chunk), BF16)] * 4
    dma = pltpu.SemaphoreType.DMA

    slabs = pltpu.VMEM((2, 2, 2, 2, 2, SLAB, 128), F32)

    def chain(route):
        left, bufs = 5, []
        for dim in ("start", *route):
            left -= dim not in LAST and dim != "start"
            lead = (len(LAST[dim]),) if dim in LAST else (2,) * left
            bufs.append(pltpu.VMEM((*lead, THIRD, 128), F32))
        return tuple(bufs)

    return pl.pallas_call(
        main_kernel,
        out_shape=tuple(jax.ShapeDtypeStruct(n.shape, F32) for n in outs),
        in_specs=[scalars] * 3 + [whole] * 3 + [pl.BlockSpec(memory_space=pl.ANY)] + [whole] * 2,
        out_specs=(whole, whole),
        scratch_shapes=[
            pltpu.VMEM((slots, tokens.shape[0]), BF16),
            *four,
            pltpu.VMEM((2, SIDE * SIDE, weight.shape[0], kv // 2), BF16),
            pltpu.VMEM((2, slots, kv // 2), F32),
            pltpu.VMEM((slots, at.shape[0]), F32),
            pltpu.VMEM((at.shape[0], width), F32),
            pltpu.VMEM(b.shape, F32),
            pltpu.VMEM((at.shape[0], 128), F32),
            slabs,
            slabs,
            slabs,
            pltpu.VMEM((width // 128, 8, 128), F32),
            pltpu.VMEM((8, 128), F32),
            pltpu.VMEM((8, 128), F32),
            tuple(chain(r) for r in ROUTES),
            dma((steps + 1,)),
            dma((steps + 1,)),
            dma((steps + 1,)),
            dma((steps + 1,)),
            dma((len(PARTS),)),
            dma((len(PARTS), 16)),
            dma((4,)),
            dma((4, 16)),
            dma((1,)),
            dma((16,)),
            dma((2,)),
            dma((SUM_SEMS,)),
            dma((SUM_SEMS,)),
        ],
        compiler_params=pltpu.CompilerParams(
            collective_id=0, has_side_effects=True, vmem_limit_bytes=62 << 20
        ),
        name="exchange_and_adapt",
    )(caps, count, bound, user, tokens, goals, weight, at, b)


def body(
    tokens,
    targets,
    row_owner_user,
    device_row_count,
    user_row_cap,
    value_weight,
    adapter_down,
    adapter_up,
    clip_norm_bound,
    down_noise,
    up_noise,
):
    sum_a, sum_b = main(
        user_row_cap, device_row_count, clip_norm_bound, row_owner_user.T, tokens, targets, value_weight,
        adapter_down.T, adapter_up, (down_noise, up_noise.T),
    )
    bound = clip_norm_bound[0]
    return sum_a + bound * down_noise, sum_b.T + bound * up_noise


def solution(mesh):
    in_specs = (
        P(BOTH, None),
        P(BOTH, None),
        P(BOTH, None),
        P(BOTH),
        P(),
        P("fsdp", None),
        P(),
        P(),
        P(),
        P(BOTH, None),
        P(None, BOTH),
    )
    out_specs = (P(BOTH, None), P(None, BOTH))
    return jax.shard_map(
        body, mesh=mesh, in_specs=in_specs, out_specs=out_specs, check_vma=False
    )
```

```python
import functools

import jax
import jax.numpy as jnp
from jax import lax
from jax.experimental import pallas as pl
from jax.experimental.pallas import tpu as pltpu
from jax.sharding import PartitionSpec as P

STEPS = 2
BOTH = ("grp", "fsdp")
MESH = pl.DeviceIdType.MESH
scale = 2.0
rate = 0.05
epsilon = 1e-06
F32 = jnp.float32
BF16 = jnp.bfloat16
SIDE = 4
ROWS_A = 64
SLAB = 72


def mm(a, b, ca, cb):
    return lax.dot_general(a, b, (((ca,), (cb,)), ((), ())), preferred_element_type=F32)


def places():
    g, f = lax.axis_index("grp"), lax.axis_index("fsdp")
    return g // 2, g % 2, f // SIDE, f % SIDE


def low(i):
    return i + 1 - 2 * (i % 2)


def mirror(i):
    return 3 - i


def bits(i, c):
    u = i // 2
    v = (i + i // 2) % 2
    return c * u + (1 - c) * v, c * v + (1 - c) * u


def sides(i, c):
    return c * mirror(i) + (1 - c) * low(i), c * low(i) + (1 - c) * mirror(i)


ROUTES = [
    ("y1", "y2", "xz"),
    ("x1", "x2", "yz"),
    ("z", "y1", "block"),
]
LAST = {
    "xz": [(0, dx, dz) for dx in range(SIDE) for dz in range(SIDE)][1:],
    "yz": [(dy, 0, dz) for dy in range(SIDE) for dz in range(SIDE)][1:],
    "block": [(n, dx, m) for n in ("same", "second") for dx in range(SIDE) for m in ("same", "low")][1:],
}
THIRD = SLAB // len(ROUTES)
FIRST_SEM = SIDE + 1
SUM_SEMS = FIRST_SEM + sum(len(LAST.get(dim, (0,))) for r in ROUTES for dim in r)


def sum_slabs(kept, taken, factor, far, chains, send, recv):
    y, c, x, z = places()

    def dev(y=y, x=x, z=z):
        return (y * 2 + c, x * SIDE + z)

    yb, xb, yn, xn = bits(y, c), bits(x, c), sides(y, c), sides(x, c)
    bit = {"y1": yb[0], "y2": yb[1], "x1": xb[0], "x2": xb[1], "z": z // 2}
    to = {
        "y1": dev(y=yn[0]),
        "y2": dev(y=yn[1]),
        "x1": dev(x=xn[0]),
        "x2": dev(x=xn[1]),
        "z": dev(z=mirror(z)),
    }
    started = []

    def go(src, dst, device):
        n = FIRST_SEM + len(started)
        d = pltpu.make_async_remote_copy(
            src_ref=src, dst_ref=dst, send_sem=send.at[n], recv_sem=recv.at[n],
            device_id=device, device_id_type=MESH,
        )
        d.start()
        started.append(d)
        return d

    near = jnp.concatenate([factor] * (THIRD // 8), axis=0)
    away = jnp.concatenate([far] * (THIRD // 8), axis=0)
    now, dims, flying = [], [], []

    def at(ref, left, dim, i):
        return ref.at[(slice(None),) * left.index(dim) + (i,)]

    def slab_of(ref, left, y, x, z):
        own = dict(zip(("y1", "y2", "x1", "x2", "z"), (*bits(y, c), *bits(x, c), z // 2)))
        return ref.at[tuple(own[d] for d in left)]

    def launch(n, step):
        dim, ref, left = ROUTES[n][step], now[n], dims[n]
        into = chains[n][step + 1]
        if dim in LAST:
            flying[n] = []
            for k, (dy, dx, dz) in enumerate(LAST[dim]):
                zz = z if dz == "same" else low(z) if dz == "low" else (z + dz) % SIDE
                yy = y if dy == "same" else yn[1] if dy == "second" else (y + dy) % SIDE
                xx = (x + dx) % SIDE
                flying[n].append(go(slab_of(ref, left, yy, xx, zz), into.at[k], dev(yy, xx, zz)))
        else:
            flying[n] = [go(at(ref, left, dim, 1 - bit[dim]), into, to[dim])]

    def land(n, step):
        dim, ref, left = ROUTES[n][step], now[n], dims[n]
        into = chains[n][step + 1]
        for d in flying[n]:
            d.wait_recv()
        if dim in LAST:
            return slab_of(ref, left, y, x, z)[...] + jnp.sum(into[...], axis=0)
        into[...] += at(ref, left, dim, bit[dim])[...]
        now[n] = into
        dims[n] = [v for v in left if v != dim]
        return None

    results = [None] * len(ROUTES)
    for n in range(len(ROUTES)):
        rows = slice(n * THIRD, (n + 1) * THIRD)
        chains[n][0][...] = near * kept[:, :, :, :, :, rows] + away * taken[:, :, :, :, :, rows]
        now.append(chains[n][0])
        dims.append(["y1", "y2", "x1", "x2", "z"])
        flying.append(None)
        launch(n, 0)
    for step in range(max(len(r) for r in ROUTES)):
        for n, route in enumerate(ROUTES):
            if step < len(route):
                results[n] = land(n, step)
                if step + 1 < len(route):
                    launch(n, step + 1)
    for d in started:
        d.wait_send()
    return jnp.concatenate(results, axis=0)


ROWS_F = 16
ROWS_G = 32
AHEAD = 2
PARTS = ((0, 176), (176, 384))
PLANES = 384
QUARTER = 32
ORDER = [(1, 0), (0, 1), (3, 0), (0, 3), (1, 1), (3, 3), (1, 3), (3, 1), (2, 0), (0, 2), (2, 1), (1, 2), (2, 3), (3, 2), (2, 2)]


def flip(i, by_low, by_mirror):
    i = i + by_low * (1 - 2 * (i % 2))
    return i + by_mirror * (3 - 2 * i)


def piece(i, h, a, b):
    i0, i1, i2, i3 = i % 2, i // 2 % 2, i // 4 % 2, i // 8
    if h == 1:
        i0, i1, i2, i3 = i1, i0, i3, i2
    return flip(a, i0, i1), flip(b, i2, i3)


def main_kernel(
    cap_ref, count_ref, bound_ref, user_ref, tok_hbm, tgt_ref, w_ref, at_hbm, b_ref,
    oa_ref, ob_ref, place_ref, tok_ref, at_ref, st, sx, rt, rx, pt, px, gt, gx, wf, acc, hid, a1, bcur, sq,
    given, kept, taken, packed, own_factor, far_factor, chains, fsend, frecv, gsend, grecv, wsend, wrecv, ysend, yrecv, csend, crecv, local, loads, ssend, srecv,
):
    y, c, x, z = places()
    g, f = y * 2 + c, x * SIDE + z
    a, b = (1 - c) * x + c * z, (1 - c) * z + c * x
    width = tok_ref.shape[1]
    kv = b_ref.shape[1]
    chunk = sx.shape[2]
    steps = width // chunk
    slots = st.shape[0]
    half = kv // 2

    def column(pos, core):
        return pos[0] * (SIDE - 3 * core) + pos[1] * (1 + 3 * core)

    f_peers = []
    for dx, dz in ORDER:
        f_peers.append((x + dx) % SIDE * SIDE + (z + dz) % SIDE)
    g_peers = []
    for dy, dc in [(1, 0), (3, 1), (3, 0), (1, 1), (2, 0), (2, 1), (0, 1)]:
        g_peers.append((y + dy) % SIDE * 2 + (c + dc) % 2)

    barrier = pltpu.get_barrier_semaphore()
    for to in f_peers:
        pl.semaphore_signal(barrier, inc=1, device_id=(g, to), device_id_type=MESH)
    for to in g_peers:
        pl.semaphore_signal(barrier, inc=1, device_id=(to, f), device_id_type=MESH)
    further = [((y + dy) % SIDE, x, (z + dz) % SIDE) for dy in range(1, SIDE) for dz in range(1, SIDE)]
    further += [(sides(y, c)[1], (x + dx) % SIDE, zz) for dx in range(1, SIDE) for zz in (z, low(z))]
    for ty, tx, tz in further:
        pl.semaphore_signal(barrier, inc=1, device_id=(ty * 2 + c, tx * SIDE + tz), device_id_type=MESH)

    early = []
    for k in range(steps):
        cols = slice(k * chunk, (k + 1) * chunk)
        early.append(pltpu.make_async_copy(tok_hbm.at[:, cols], tok_ref.at[:, cols], loads.at[k]))
    early.append(pltpu.make_async_copy(at_hbm, at_ref, loads.at[steps]))
    for d in early:
        d.start()

    keep = []
    for n in range(2):
        keep.append(pltpu.make_async_copy(w_ref.at[:, n * half : (n + 1) * half], wf.at[n, f], local.at[n]))
        keep[-1].start()

    user = user_ref[...]
    per = user.shape[1]
    u_i = lax.broadcasted_iota(jnp.int32, (per, per), 0)
    v_i = lax.broadcasted_iota(jnp.int32, (per, per), 1)
    named = jnp.where(lax.broadcasted_iota(jnp.int32, (128, per), 0) == user, 1.0, 0.0)
    above = jnp.where(u_i < v_i, 1.0, 0.0).astype(BF16)
    rank = jnp.sum(mm(named.astype(BF16), above, 1, 0) * named, axis=0, keepdims=True).astype(jnp.int32)
    slot = (user & 15) * ROWS_F + (user >> 4) * 2 + rank
    place_ref[...] = jnp.where(lax.broadcasted_iota(jnp.int32, (slots, per), 0) == slot, 1.0, 0.0).astype(BF16)
    count = count_ref[0]
    flags = jnp.where(lax.broadcasted_iota(jnp.int32, (per, 128), 0) < count, 1.0, 0.0).astype(BF16)
    place = place_ref[...]
    n_i = lax.broadcasted_iota(jnp.int32, (slots, slots), 0)
    o_i = lax.broadcasted_iota(jnp.int32, (slots, slots), 1)
    old = ((n_i >> 1) & 15) * 16 + (n_i >> 5) * 2 + (n_i & 1)
    turn = jnp.where(o_i == old, 1.0, 0.0).astype(BF16)

    def bufs(k):
        if k == 0:
            return st, rt, pt, gt
        return sx.at[k - 1], rx.at[k - 1], px.at[k - 1], gx.at[k - 1]

    def rows_f(i):
        return pl.ds(pl.multiple_of(i * ROWS_F, ROWS_F), ROWS_F)

    def rows_g(i):
        return pl.ds(pl.multiple_of(i * ROWS_G, ROWS_G), ROWS_G)

    def place_rows(k):
        s = bufs(k)[0]
        if k == 0:
            s[:, :kv] = mm(place, tgt_ref[...], 1, 0).astype(BF16)
            s[:, kv:] = mm(place, flags, 1, 0).astype(BF16)
        else:
            early[k - 1].wait()
            s[...] = mm(place, tok_ref[:, (k - 1) * chunk : k * chunk], 1, 0).astype(BF16)

    def start_f(k):
        s, r, _, _ = bufs(k)
        for to in f_peers:
            pltpu.make_async_remote_copy(
                src_ref=s.at[rows_f(to)], dst_ref=r.at[rows_f(f)], send_sem=fsend.at[k], recv_sem=frecv.at[k],
                device_id=(g, to), device_id_type=MESH,
            ).start()
        r[rows_f(f), :] = s[rows_f(f), :]

    def turn_rows(k):
        _, r, p, q = bufs(k)
        most = r.at[: slots - ROWS_F]
        pltpu.make_async_copy(most, most, frecv.at[k]).wait()
        p[...] = mm(turn, r[...], 1, 0).astype(BF16)
        for to in g_peers:
            pltpu.make_async_remote_copy(
                src_ref=p.at[rows_g(to)], dst_ref=q.at[rows_g(g)], send_sem=gsend.at[k], recv_sem=grecv.at[k],
                device_id=(to, f), device_id_type=MESH,
            ).start()
        q[rows_g(g), :] = p[rows_g(g), :]

    def end_g(k):
        q = bufs(k)[3]
        most = q.at[: slots - ROWS_G]
        pltpu.make_async_copy(most, most, grecv.at[k]).wait()

    def send(src, dst, ssem, rsem, device):
        pltpu.make_async_remote_copy(
            src_ref=src, dst_ref=dst, send_sem=ssem, recv_sem=rsem, device_id=device, device_id_type=MESH
        ).start()

    def await_bytes(ref, sem):
        pltpu.make_async_copy(ref, ref, sem).wait()

    yn = sides(y, c)
    beyond = sides(yn[1], c)[0]
    my_half = pl.ds(pl.multiple_of(c * half, half), half)

    def quarter(q):
        return pl.ds(pl.multiple_of(PLANES + q * QUARTER, 16), QUARTER)

    def col_of(i, h=0):
        return column(piece(i, h, a, b), c)

    def pass_on(i, h):
        rows = slice(*PARTS[h])
        ref = wf.at[c, col_of(i, h), rows]
        src = ref
        if i == 0:
            src = w_ref.at[rows, my_half]
        else:
            await_bytes(ref, wrecv.at[h, i])
        for n in range(i.bit_length(), 4):
            send(src, ref, wsend.at[h], wrecv.at[h, (1 << n) + i], (g, col_of(1 << n, h)))

    def pass_quarter(i, level):
        ref = wf.at[c, col_of(i), quarter(y)]
        src = ref
        if level == 0:
            src = w_ref.at[quarter(y), my_half]
        else:
            await_bytes(ref, yrecv.at[0, i])
        for n in range(level, 4):
            send(src, ref, ysend.at[0], yrecv.at[0, (1 << n) + i], (g, col_of(1 << n)))
        if level:
            for n in range(2):
                send(ref, ref, ysend.at[1 + n], yrecv.at[1 + n, i], (yn[n] * 2 + c, f))

    def relay(i):
        ref = wf.at[c, col_of(i), quarter(yn[0])]
        await_bytes(ref, yrecv.at[1, i])
        send(ref, ref, ysend.at[3], yrecv.at[3, i], (yn[1] * 2 + c, f))

    def add(n, col):
        depth = w_ref.shape[0]
        per = chunk // depth
        x_cols = gx[col // per, :, pl.ds(pl.multiple_of(col % per * depth, depth), depth)]
        acc[n] += mm(x_cols, wf[n, col], 1, 0)

    def add_other(i):
        col = column(piece(i, 0, b, a), 1 - c)
        await_bytes(wf.at[1 - c, col], crecv.at[i])
        add(1 - c, col)

    place_rows(0)
    pl.semaphore_wait(barrier, len(f_peers) + len(g_peers) + len(further))
    start_f(0)
    place_rows(1)
    start_f(1)
    acc[...] = jnp.zeros_like(acc)
    hid[...] = jnp.zeros_like(hid)
    both = range(len(PARTS))
    def last_quarters():
        @pl.loop(8, 16)
        def _(i):
            pass_quarter(i, 4)

    def relays(lo, hi):
        @pl.loop(lo, hi)
        def _(i):
            relay(i)

    todo = {
        1: lambda: pass_quarter(0, 0),
        2: lambda: pass_quarter(1, 1),
        3: lambda: [pass_quarter(i, 2) for i in (2, 3)],
        4: lambda: [pass_quarter(i, 3) for i in (4, 5, 6, 7)],
        5: lambda: [pass_on(0, h) for h in both] + [last_quarters()],
        7: lambda: [pass_on(1, h) for h in both] + [relays(1, 8)],
        8: lambda: [relays(8, 16)],
        9: lambda: [pass_on(i, h) for i in (2, 3) for h in both],
        10: lambda: [pass_on(i, h) for i in (4, 5, 6, 7) for h in both],
    }
    for k in range(1, steps + 1 + AHEAD):
        if 1 < k <= steps:
            place_rows(k)
            start_f(k)
        if k >= AHEAD:
            turn_rows(k - AHEAD)
        if k in todo:
            todo[k]()

    early[steps].wait()
    end_g(0)
    for k in range(1, steps + 1):
        end_g(k)
        hid[...] += mm(gx[k - 1], at_ref[:, (k - 1) * chunk : k * chunk], 1, 1)
    for d in keep:
        d.wait()
    for n in range(2):
        add(n, f)

    @pl.loop(1, 16)
    def _(i):
        col = col_of(i)
        twin = i % 2 * 2 + i // 2 % 2 + i // 4 % 2 * 8 + i // 8 * 4

        @pl.when(i >= 8)
        def _():
            await_bytes(wf.at[c, col, slice(*PARTS[0])], wrecv.at[0, i])

        @pl.when(twin >= 8)
        def _():
            await_bytes(wf.at[c, col, slice(*PARTS[1])], wrecv.at[1, twin])

        await_bytes(wf.at[c, col, quarter(yn[1])], yrecv.at[2, i])
        await_bytes(wf.at[c, col, quarter(beyond)], yrecv.at[3, i])
        shard = wf.at[c, col]
        send(shard, shard, csend.at[0], crecv.at[i], (y * 2 + 1 - c, f))
        add(c, col)

        @pl.when(i >= 3)
        def _():
            add_other(i - 2)

    add_other(14)
    add_other(15)

    cap, bound = cap_ref[g * SIDE * SIDE + f].astype(F32), bound_ref[0]
    used = gt[:, kv:]
    before = jnp.where(o_i < n_i, 1.0, 0.0).astype(BF16)
    earlier = mm(before, used, 1, 0)
    live = jnp.where((used.astype(F32) > 0.5) & (earlier < cap), 1.0 / cap, 0.0)
    live = jnp.concatenate([live] * (kv // live.shape[1]), axis=1)
    base = jnp.concatenate([acc[0], acc[1]], axis=1) - gt[:, :kv].astype(F32)

    def part(k):
        return pl.ds(pl.multiple_of(k * chunk, chunk), chunk)

    def errors(h, b16):
        r = (live * (base + scale * mm(h, b16, 1, 0))).astype(BF16)
        return mm(r, b16, 1, 1).astype(BF16), scale * mm(h, r, 0, 0)

    b0 = b_ref[...]
    back, grad_b = errors(hid[...].astype(BF16), b0)
    bcur[...] = b0.astype(F32) - rate * grad_b
    hid[...] = jnp.zeros_like(hid)

    @pl.loop(0, steps)
    def _(k):
        rows = gx[k]
        now = at_ref[:, part(k)].astype(F32) - rate * (scale * mm(back, rows, 0, 0))
        a1[:, part(k)] = now
        hid[...] += mm(rows, now.astype(BF16), 1, 1)

    back2, grad_b2 = errors(hid[...].astype(BF16), bcur[...].astype(BF16))
    delta_b = (bcur[...] - rate * grad_b2) - b0.astype(F32)
    sq[...] = jnp.zeros_like(sq)

    bt = delta_b.T.reshape(width // 128, 16, ROWS_A)
    packed[...] = jnp.concatenate([bt[:, :8, :], bt[:, 8:, :]], axis=2)
    other_core = (y * 2 + 1 - c, f)

    def to_core(src, dst, n):
        return pltpu.make_async_remote_copy(
            src_ref=src, dst_ref=dst, send_sem=ssend.at[n], recv_sem=srecv.at[n],
            device_id=other_core, device_id_type=MESH,
        )

    first = []
    for to_far in (True, False):
        core = 1 - c if to_far else c
        slabs = given if to_far else kept
        for yy in range(SIDE):
            k = yy * 2 + core
            d = (a1[:, part(k)] - rate * (scale * mm(back2, gx[k], 0, 0))) - at_ref[:, part(k)].astype(F32)
            sq[...] += jnp.sum((d * d).reshape(d.shape[0], chunk // 128, 128), axis=1)
            y1, y2 = bits(yy, core)
            for p in range(chunk // 128):
                x1, x2 = bits(p // 2, core)
                slabs[y1, y2, x1, x2, p % 2, :ROWS_A, :] = d[:, p * 128 : (p + 1) * 128]
                slabs[y1, y2, x1, x2, p % 2, ROWS_A:, :] = packed[k * (chunk // 128) + p]
            if to_far:
                first.append(to_core(given.at[y1, y2], taken.at[y1, y2], yy))
                first[-1].start()

    total = jnp.sum(sq[...]) + jnp.sum(delta_b * delta_b)
    own_factor[...] = jnp.minimum(1.0, bound / jnp.sqrt(jnp.broadcast_to(total, (8, 128)) + epsilon))
    first.append(to_core(own_factor, far_factor, SIDE))
    first[-1].start()
    for d in first:
        d.wait_recv()
    slab = sum_slabs(kept, taken, own_factor[...], far_factor[...], chains, ssend, srecv)
    val = jnp.where(z % 2 == 1, slab[:, ROWS_A:], slab[:, :ROWS_A])
    oa_ref[...] = val[:ROWS_A].T
    ob_ref[...] = val[ROWS_A:]
    for d in first:
        d.wait_send()

    for k in range(steps + 1):
        s, _, p, _ = bufs(k)
        most = s.at[: slots - ROWS_F]
        pltpu.make_async_copy(most, most, fsend.at[k]).wait()
        most = p.at[: slots - ROWS_G]
        pltpu.make_async_copy(most, most, gsend.at[k]).wait()
    for h in both:
        await_bytes(wf.at[0, :15, slice(*PARTS[h])], wsend.at[h])
    for n in range(4):
        await_bytes(wf.at[0, :15, :QUARTER], ysend.at[n])
    await_bytes(wf.at[0, :15], csend.at[0])


def main(caps, count, bound, user, tokens, goals, weight, at, b, outs):
    width, kv = tokens.shape[1], b.shape[1]
    slots = ROWS_F * SIDE * SIDE
    chunk = 1024
    steps = width // chunk
    extra = kv + 128
    whole = pl.BlockSpec(memory_space=pltpu.VMEM)
    scalars = pl.BlockSpec(memory_space=pltpu.SMEM)
    left = pl.BlockSpec(memory_space=pl.ANY)
    four = [pltpu.VMEM((slots, extra), BF16), pltpu.VMEM((steps, slots, chunk), BF16)] * 4
    dma = pltpu.SemaphoreType.DMA

    slabs = pltpu.VMEM((2, 2, 2, 2, 2, SLAB, 128), F32)

    def chain(route):
        left, bufs = 5, []
        for dim in ("start", *route):
            left -= dim not in LAST and dim != "start"
            lead = (len(LAST[dim]),) if dim in LAST else (2,) * left
            bufs.append(pltpu.VMEM((*lead, THIRD, 128), F32))
        return tuple(bufs)

    return pl.pallas_call(
        main_kernel,
        out_shape=tuple(jax.ShapeDtypeStruct(n.shape, F32) for n in outs),
        in_specs=[scalars] * 3 + [whole, left, whole, left, left, whole],
        out_specs=(whole, whole),
        scratch_shapes=[
            pltpu.VMEM((slots, tokens.shape[0]), BF16),
            pltpu.VMEM(tokens.shape, BF16),
            pltpu.VMEM(at.shape, BF16),
            *four,
            pltpu.VMEM((2, SIDE * SIDE, weight.shape[0], kv // 2), BF16),
            pltpu.VMEM((2, slots, kv // 2), F32),
            pltpu.VMEM((slots, at.shape[0]), F32),
            pltpu.VMEM((at.shape[0], width), F32),
            pltpu.VMEM(b.shape, F32),
            pltpu.VMEM((at.shape[0], 128), F32),
            slabs,
            slabs,
            slabs,
            pltpu.VMEM((width // 128, 8, 128), F32),
            pltpu.VMEM((8, 128), F32),
            pltpu.VMEM((8, 128), F32),
            tuple(chain(r) for r in ROUTES),
            dma((steps + 1,)),
            dma((steps + 1,)),
            dma((steps + 1,)),
            dma((steps + 1,)),
            dma((len(PARTS),)),
            dma((len(PARTS), 16)),
            dma((4,)),
            dma((4, 16)),
            dma((1,)),
            dma((16,)),
            dma((2,)),
            dma((steps + 1,)),
            dma((SUM_SEMS,)),
            dma((SUM_SEMS,)),
        ],
        compiler_params=pltpu.CompilerParams(
            collective_id=0, has_side_effects=True, vmem_limit_bytes=62 << 20
        ),
        name="exchange_and_adapt",
    )(caps, count, bound, user, tokens, goals, weight, at, b)


def body(
    tokens,
    targets,
    row_owner_user,
    device_row_count,
    user_row_cap,
    value_weight,
    adapter_down,
    adapter_up,
    clip_norm_bound,
    down_noise,
    up_noise,
):
    sum_a, sum_b = main(
        user_row_cap, device_row_count, clip_norm_bound, row_owner_user.T, tokens, targets, value_weight,
        adapter_down.T, adapter_up, (down_noise, up_noise.T),
    )
    bound = clip_norm_bound[0]
    return sum_a + bound * down_noise, sum_b.T + bound * up_noise


def solution(mesh):
    in_specs = (
        P(BOTH, None),
        P(BOTH, None),
        P(BOTH, None),
        P(BOTH),
        P(),
        P("fsdp", None),
        P(),
        P(),
        P(),
        P(BOTH, None),
        P(None, BOTH),
    )
    out_specs = (P(BOTH, None), P(None, BOTH))
    return jax.shard_map(
        body, mesh=mesh, in_specs=in_specs, out_specs=out_specs, check_vma=False
    )
```

```python
import functools

import jax
import jax.numpy as jnp
from jax import lax
from jax.experimental import pallas as pl
from jax.experimental.pallas import tpu as pltpu
from jax.sharding import PartitionSpec as P

STEPS = 2
BOTH = ("grp", "fsdp")
MESH = pl.DeviceIdType.MESH
scale = 2.0
rate = 0.05
epsilon = 1e-06
F32 = jnp.float32
BF16 = jnp.bfloat16
SIDE = 4
ROWS_A = 64
SLAB = 72


def mm(a, b, ca, cb):
    return lax.dot_general(a, b, (((ca,), (cb,)), ((), ())), preferred_element_type=F32)


def places():
    g, f = lax.axis_index("grp"), lax.axis_index("fsdp")
    return g // 2, g % 2, f // SIDE, f % SIDE


def low(i):
    return i + 1 - 2 * (i % 2)


def mirror(i):
    return 3 - i


def bits(i, c):
    u = i // 2
    v = (i + i // 2) % 2
    return c * u + (1 - c) * v, c * v + (1 - c) * u


def sides(i, c):
    return c * mirror(i) + (1 - c) * low(i), c * low(i) + (1 - c) * mirror(i)


ROUTES = [
    ("y1", "y2", "xz"),
    ("x1", "x2", "yz"),
    ("z", "y1", "block"),
]
LAST = {
    "xz": [(0, dx, dz) for dx in range(SIDE) for dz in range(SIDE)][1:],
    "yz": [(dy, 0, dz) for dy in range(SIDE) for dz in range(SIDE)][1:],
    "block": [(n, dx, m) for n in ("same", "second") for dx in range(SIDE) for m in ("same", "low")][1:],
}
THIRD = SLAB // len(ROUTES)
FIRST_SEM = SIDE + 1
SUM_SEMS = FIRST_SEM + sum(len(LAST.get(dim, (0,))) for r in ROUTES for dim in r)


def sum_slabs(kept, taken, factor, far, chains, send, recv):
    y, c, x, z = places()

    def dev(y=y, x=x, z=z):
        return (y * 2 + c, x * SIDE + z)

    yb, xb, yn, xn = bits(y, c), bits(x, c), sides(y, c), sides(x, c)
    bit = {"y1": yb[0], "y2": yb[1], "x1": xb[0], "x2": xb[1], "z": z // 2}
    to = {
        "y1": dev(y=yn[0]),
        "y2": dev(y=yn[1]),
        "x1": dev(x=xn[0]),
        "x2": dev(x=xn[1]),
        "z": dev(z=mirror(z)),
    }
    started = []

    def go(src, dst, device):
        n = FIRST_SEM + len(started)
        d = pltpu.make_async_remote_copy(
            src_ref=src, dst_ref=dst, send_sem=send.at[n], recv_sem=recv.at[n],
            device_id=device, device_id_type=MESH,
        )
        d.start()
        started.append(d)
        return d

    near = jnp.concatenate([factor] * (THIRD // 8), axis=0)
    away = jnp.concatenate([far] * (THIRD // 8), axis=0)
    now, dims, flying = [], [], []

    def at(ref, left, dim, i):
        return ref.at[(slice(None),) * left.index(dim) + (i,)]

    def slab_of(ref, left, y, x, z):
        own = dict(zip(("y1", "y2", "x1", "x2", "z"), (*bits(y, c), *bits(x, c), z // 2)))
        return ref.at[tuple(own[d] for d in left)]

    def launch(n, step):
        dim, ref, left = ROUTES[n][step], now[n], dims[n]
        into = chains[n][step + 1]
        if dim in LAST:
            flying[n] = []
            for k, (dy, dx, dz) in enumerate(LAST[dim]):
                zz = z if dz == "same" else low(z) if dz == "low" else (z + dz) % SIDE
                yy = y if dy == "same" else yn[1] if dy == "second" else (y + dy) % SIDE
                xx = (x + dx) % SIDE
                flying[n].append(go(slab_of(ref, left, yy, xx, zz), into.at[k], dev(yy, xx, zz)))
        else:
            flying[n] = [go(at(ref, left, dim, 1 - bit[dim]), into, to[dim])]

    def land(n, step):
        dim, ref, left = ROUTES[n][step], now[n], dims[n]
        into = chains[n][step + 1]
        for d in flying[n]:
            d.wait_recv()
        if dim in LAST:
            return slab_of(ref, left, y, x, z)[...] + jnp.sum(into[...], axis=0)
        into[...] += at(ref, left, dim, bit[dim])[...]
        now[n] = into
        dims[n] = [v for v in left if v != dim]
        return None

    results = [None] * len(ROUTES)
    for n in range(len(ROUTES)):
        rows = slice(n * THIRD, (n + 1) * THIRD)
        chains[n][0][...] = near * kept[:, :, :, :, :, rows] + away * taken[:, :, :, :, :, rows]
        now.append(chains[n][0])
        dims.append(["y1", "y2", "x1", "x2", "z"])
        flying.append(None)
        launch(n, 0)
    for step in range(max(len(r) for r in ROUTES)):
        for n, route in enumerate(ROUTES):
            if step < len(route):
                results[n] = land(n, step)
                if step + 1 < len(route):
                    launch(n, step + 1)
    for d in started:
        d.wait_send()
    return jnp.concatenate(results, axis=0)


ROWS_F = 16
ROWS_G = 32
AHEAD = 2
PARTS = ((0, 176), (176, 384))
PLANES = 384
QUARTER = 32
ORDER = [(1, 0), (0, 1), (3, 0), (0, 3), (1, 1), (3, 3), (1, 3), (3, 1), (2, 0), (0, 2), (2, 1), (1, 2), (2, 3), (3, 2), (2, 2)]


def flip(i, by_low, by_mirror):
    i = i + by_low * (1 - 2 * (i % 2))
    return i + by_mirror * (3 - 2 * i)


def piece(i, h, a, b):
    i0, i1, i2, i3 = i % 2, i // 2 % 2, i // 4 % 2, i // 8
    if h == 1:
        i0, i1, i2, i3 = i1, i0, i3, i2
    return flip(a, i0, i1), flip(b, i2, i3)


def main_kernel(
    cap_ref, count_ref, bound_ref, user_ref, tok_hbm, tgt_ref, w_ref, at_hbm, b_ref,
    oa_ref, ob_ref, place_ref, tok_ref, at_ref, st, sx, rt, rx, pt, px, gt, gx, wf, acc, hid, a1, bcur, sq,
    given, kept, taken, packed, own_factor, far_factor, chains, fsend, frecv, gsend, grecv, wsend, wrecv, ysend, yrecv, csend, crecv, local, loads, ssend, srecv,
):
    y, c, x, z = places()
    g, f = y * 2 + c, x * SIDE + z
    a, b = (1 - c) * x + c * z, (1 - c) * z + c * x
    width = tok_ref.shape[1]
    kv = b_ref.shape[1]
    chunk = sx.shape[2]
    steps = width // chunk
    slots = st.shape[0]
    half = kv // 2

    def column(pos, core):
        return pos[0] * (SIDE - 3 * core) + pos[1] * (1 + 3 * core)

    f_peers = []
    for dx, dz in ORDER:
        f_peers.append((x + dx) % SIDE * SIDE + (z + dz) % SIDE)
    g_peers = []
    for dy, dc in [(1, 0), (3, 1), (3, 0), (1, 1), (2, 0), (2, 1), (0, 1)]:
        g_peers.append((y + dy) % SIDE * 2 + (c + dc) % 2)

    barrier = pltpu.get_barrier_semaphore()
    for to in f_peers:
        pl.semaphore_signal(barrier, inc=1, device_id=(g, to), device_id_type=MESH)
    for to in g_peers:
        pl.semaphore_signal(barrier, inc=1, device_id=(to, f), device_id_type=MESH)
    further = [((y + dy) % SIDE, x, (z + dz) % SIDE) for dy in range(1, SIDE) for dz in range(1, SIDE)]
    further += [(sides(y, c)[1], (x + dx) % SIDE, zz) for dx in range(1, SIDE) for zz in (z, low(z))]
    for ty, tx, tz in further:
        pl.semaphore_signal(barrier, inc=1, device_id=(ty * 2 + c, tx * SIDE + tz), device_id_type=MESH)

    early = []
    for k in range(steps):
        cols = slice(k * chunk, (k + 1) * chunk)
        early.append(pltpu.make_async_copy(tok_hbm.at[:, cols], tok_ref.at[:, cols], loads.at[k]))
    early.append(pltpu.make_async_copy(at_hbm, at_ref, loads.at[steps]))
    for d in early:
        d.start()

    keep = []
    for n in range(2):
        keep.append(pltpu.make_async_copy(w_ref.at[:, n * half : (n + 1) * half], wf.at[n, f], local.at[n]))
        keep[-1].start()

    user = user_ref[...]
    per = user.shape[1]
    u_i = lax.broadcasted_iota(jnp.int32, (per, per), 0)
    v_i = lax.broadcasted_iota(jnp.int32, (per, per), 1)
    named = jnp.where(lax.broadcasted_iota(jnp.int32, (128, per), 0) == user, 1.0, 0.0)
    above = jnp.where(u_i < v_i, 1.0, 0.0).astype(BF16)
    rank = jnp.sum(mm(named.astype(BF16), above, 1, 0) * named, axis=0, keepdims=True).astype(jnp.int32)
    slot = (user & 15) * ROWS_F + (user >> 4) * 2 + rank
    place_ref[...] = jnp.where(lax.broadcasted_iota(jnp.int32, (slots, per), 0) == slot, 1.0, 0.0).astype(BF16)
    count = count_ref[0]
    flags = jnp.where(lax.broadcasted_iota(jnp.int32, (per, 128), 0) < count, 1.0, 0.0).astype(BF16)
    place = place_ref[...]
    n_i = lax.broadcasted_iota(jnp.int32, (slots, slots), 0)
    o_i = lax.broadcasted_iota(jnp.int32, (slots, slots), 1)
    old = ((n_i >> 1) & 15) * 16 + (n_i >> 5) * 2 + (n_i & 1)
    turn = jnp.where(o_i == old, 1.0, 0.0).astype(BF16)

    def bufs(k):
        if k == 0:
            return st, rt, pt, gt
        return sx.at[k - 1], rx.at[k - 1], px.at[k - 1], gx.at[k - 1]

    def rows_f(i):
        return pl.ds(pl.multiple_of(i * ROWS_F, ROWS_F), ROWS_F)

    def rows_g(i):
        return pl.ds(pl.multiple_of(i * ROWS_G, ROWS_G), ROWS_G)

    def place_rows(k):
        s = bufs(k)[0]
        if k == 0:
            s[:, :kv] = mm(place, tgt_ref[...], 1, 0).astype(BF16)
            s[:, kv:] = mm(place, flags, 1, 0).astype(BF16)
        else:
            early[k - 1].wait()
            s[...] = mm(place, tok_ref[:, (k - 1) * chunk : k * chunk], 1, 0).astype(BF16)

    def start_f(k):
        s, r, _, _ = bufs(k)
        for to in f_peers:
            pltpu.make_async_remote_copy(
                src_ref=s.at[rows_f(to)], dst_ref=r.at[rows_f(f)], send_sem=fsend.at[k], recv_sem=frecv.at[k],
                device_id=(g, to), device_id_type=MESH,
            ).start()
        r[rows_f(f), :] = s[rows_f(f), :]

    def turn_rows(k):
        _, r, p, q = bufs(k)
        most = r.at[: slots - ROWS_F]
        pltpu.make_async_copy(most, most, frecv.at[k]).wait()
        p[...] = mm(turn, r[...], 1, 0).astype(BF16)
        for to in g_peers:
            pltpu.make_async_remote_copy(
                src_ref=p.at[rows_g(to)], dst_ref=q.at[rows_g(g)], send_sem=gsend.at[k], recv_sem=grecv.at[k],
                device_id=(to, f), device_id_type=MESH,
            ).start()
        q[rows_g(g), :] = p[rows_g(g), :]

    def end_g(k):
        q = bufs(k)[3]
        most = q.at[: slots - ROWS_G]
        pltpu.make_async_copy(most, most, grecv.at[k]).wait()

    def send(src, dst, ssem, rsem, device):
        pltpu.make_async_remote_copy(
            src_ref=src, dst_ref=dst, send_sem=ssem, recv_sem=rsem, device_id=device, device_id_type=MESH
        ).start()

    def await_bytes(ref, sem):
        pltpu.make_async_copy(ref, ref, sem).wait()

    yn = sides(y, c)
    beyond = sides(yn[1], c)[0]
    my_half = pl.ds(pl.multiple_of(c * half, half), half)

    def quarter(q):
        return pl.ds(pl.multiple_of(PLANES + q * QUARTER, 16), QUARTER)

    def col_of(i, h=0):
        return column(piece(i, h, a, b), c)

    def pass_on(i, h):
        rows = slice(*PARTS[h])
        ref = wf.at[c, col_of(i, h), rows]
        src = ref
        if i == 0:
            src = w_ref.at[rows, my_half]
        else:
            await_bytes(ref, wrecv.at[h, i])
        for n in range(i.bit_length(), 4):
            send(src, ref, wsend.at[h], wrecv.at[h, (1 << n) + i], (g, col_of(1 << n, h)))

    def pass_quarter(i, level):
        ref = wf.at[c, col_of(i), quarter(y)]
        src = ref
        if level == 0:
            src = w_ref.at[quarter(y), my_half]
        else:
            await_bytes(ref, yrecv.at[0, i])
        for n in range(level, 4):
            send(src, ref, ysend.at[0], yrecv.at[0, (1 << n) + i], (g, col_of(1 << n)))
        if level:
            for n in range(2):
                send(ref, ref, ysend.at[1 + n], yrecv.at[1 + n, i], (yn[n] * 2 + c, f))

    def relay(i):
        ref = wf.at[c, col_of(i), quarter(yn[0])]
        await_bytes(ref, yrecv.at[1, i])
        send(ref, ref, ysend.at[3], yrecv.at[3, i], (yn[1] * 2 + c, f))

    def add(n, col):
        depth = w_ref.shape[0]
        per = chunk // depth
        x_cols = gx[col // per, :, pl.ds(pl.multiple_of(col % per * depth, depth), depth)]
        acc[n] += mm(x_cols, wf[n, col], 1, 0)

    def add_other(i):
        col = column(piece(i, 0, b, a), 1 - c)
        await_bytes(wf.at[1 - c, col], crecv.at[i])
        add(1 - c, col)

    place_rows(0)
    pl.semaphore_wait(barrier, len(f_peers) + len(g_peers) + len(further))
    start_f(0)
    place_rows(1)
    start_f(1)
    acc[...] = jnp.zeros_like(acc)
    hid[...] = jnp.zeros_like(hid)
    both = range(len(PARTS))
    def last_quarters():
        @pl.loop(8, 16)
        def _(i):
            pass_quarter(i, 4)

    def relays(lo, hi):
        @pl.loop(lo, hi)
        def _(i):
            relay(i)

    todo = {
        1: lambda: pass_quarter(0, 0),
        2: lambda: pass_quarter(1, 1),
        3: lambda: [pass_quarter(i, 2) for i in (2, 3)],
        4: lambda: [pass_quarter(i, 3) for i in (4, 5, 6, 7)],
        5: lambda: [pass_on(0, h) for h in both] + [last_quarters()],
        7: lambda: [pass_on(1, h) for h in both] + [relays(1, 8)],
        8: lambda: [relays(8, 16)],
        9: lambda: [pass_on(i, h) for i in (2, 3) for h in both],
        10: lambda: [pass_on(i, h) for i in (4, 5, 6, 7) for h in both],
    }
    for k in range(1, steps + 1 + AHEAD):
        if 1 < k <= steps:
            place_rows(k)
            start_f(k)
        if k >= AHEAD:
            turn_rows(k - AHEAD)
        if k in todo:
            todo[k]()

    early[steps].wait()
    end_g(0)
    for k in range(1, steps + 1):
        end_g(k)
        hid[...] += mm(gx[k - 1], at_ref[:, (k - 1) * chunk : k * chunk], 1, 1)
    for d in keep:
        d.wait()
    for n in range(2):
        add(n, f)

    @pl.loop(1, 16)
    def _(i):
        col = col_of(i)
        twin = i % 2 * 2 + i // 2 % 2 + i // 4 % 2 * 8 + i // 8 * 4

        @pl.when(i >= 8)
        def _():
            await_bytes(wf.at[c, col, slice(*PARTS[0])], wrecv.at[0, i])

        @pl.when(twin >= 8)
        def _():
            await_bytes(wf.at[c, col, slice(*PARTS[1])], wrecv.at[1, twin])

        await_bytes(wf.at[c, col, quarter(yn[1])], yrecv.at[2, i])
        await_bytes(wf.at[c, col, quarter(beyond)], yrecv.at[3, i])
        shard = wf.at[c, col]
        send(shard, shard, csend.at[0], crecv.at[i], (y * 2 + 1 - c, f))
        add(c, col)

        @pl.when(i >= 3)
        def _():
            add_other(i - 2)

    add_other(14)
    add_other(15)

    cap, bound = cap_ref[g * SIDE * SIDE + f].astype(F32), bound_ref[0]
    used = gt[:, kv:]
    before = jnp.where(o_i < n_i, 1.0, 0.0).astype(BF16)
    earlier = mm(before, used, 1, 0)
    live = jnp.where((used.astype(F32) > 0.5) & (earlier < cap), 1.0 / cap, 0.0)
    live = jnp.concatenate([live] * (kv // live.shape[1]), axis=1)
    base = jnp.concatenate([acc[0], acc[1]], axis=1) - gt[:, :kv].astype(F32)

    def part(k):
        return pl.ds(pl.multiple_of(k * chunk, chunk), chunk)

    def errors(h, b16):
        r = (live * (base + scale * mm(h, b16, 1, 0))).astype(BF16)
        return mm(r, b16, 1, 1).astype(BF16), scale * mm(h, r, 0, 0)

    b0 = b_ref[...]
    back, grad_b = errors(hid[...].astype(BF16), b0)
    bcur[...] = b0.astype(F32) - rate * grad_b
    hid[...] = jnp.zeros_like(hid)

    @pl.loop(0, steps, unroll=4)
    def _(k):
        rows = gx[k]
        now = at_ref[:, part(k)].astype(F32) - rate * (scale * mm(back, rows, 0, 0))
        a1[:, part(k)] = now
        hid[...] += mm(rows, now.astype(BF16), 1, 1)

    back2, grad_b2 = errors(hid[...].astype(BF16), bcur[...].astype(BF16))
    delta_b = (bcur[...] - rate * grad_b2) - b0.astype(F32)
    sq[...] = jnp.zeros_like(sq)

    bt = delta_b.T.reshape(width // 128, 16, ROWS_A)
    packed[...] = jnp.concatenate([bt[:, :8, :], bt[:, 8:, :]], axis=2)
    other_core = (y * 2 + 1 - c, f)

    def to_core(src, dst, n):
        return pltpu.make_async_remote_copy(
            src_ref=src, dst_ref=dst, send_sem=ssend.at[n], recv_sem=srecv.at[n],
            device_id=other_core, device_id_type=MESH,
        )

    first = []
    for to_far in (True, False):
        core = 1 - c if to_far else c
        slabs = given if to_far else kept
        for yy in range(SIDE):
            k = yy * 2 + core
            d = (a1[:, part(k)] - rate * (scale * mm(back2, gx[k], 0, 0))) - at_ref[:, part(k)].astype(F32)
            sq[...] += jnp.sum((d * d).reshape(d.shape[0], chunk // 128, 128), axis=1)
            y1, y2 = bits(yy, core)
            for p in range(chunk // 128):
                x1, x2 = bits(p // 2, core)
                slabs[y1, y2, x1, x2, p % 2, :ROWS_A, :] = d[:, p * 128 : (p + 1) * 128]
                slabs[y1, y2, x1, x2, p % 2, ROWS_A:, :] = packed[k * (chunk // 128) + p]
            if to_far:
                first.append(to_core(given.at[y1, y2], taken.at[y1, y2], yy))
                first[-1].start()

    total = jnp.sum(sq[...]) + jnp.sum(delta_b * delta_b)
    own_factor[...] = jnp.minimum(1.0, bound / jnp.sqrt(jnp.broadcast_to(total, (8, 128)) + epsilon))
    first.append(to_core(own_factor, far_factor, SIDE))
    first[-1].start()
    for d in first:
        d.wait_recv()
    slab = sum_slabs(kept, taken, own_factor[...], far_factor[...], chains, ssend, srecv)
    val = jnp.where(z % 2 == 1, slab[:, ROWS_A:], slab[:, :ROWS_A])
    oa_ref[...] = val[:ROWS_A].T
    ob_ref[...] = val[ROWS_A:]
    for d in first:
        d.wait_send()

    for k in range(steps + 1):
        s, _, p, _ = bufs(k)
        most = s.at[: slots - ROWS_F]
        pltpu.make_async_copy(most, most, fsend.at[k]).wait()
        most = p.at[: slots - ROWS_G]
        pltpu.make_async_copy(most, most, gsend.at[k]).wait()
    for h in both:
        await_bytes(wf.at[0, :15, slice(*PARTS[h])], wsend.at[h])
    for n in range(4):
        await_bytes(wf.at[0, :15, :QUARTER], ysend.at[n])
    await_bytes(wf.at[0, :15], csend.at[0])


def main(caps, count, bound, user, tokens, goals, weight, at, b, outs):
    width, kv = tokens.shape[1], b.shape[1]
    slots = ROWS_F * SIDE * SIDE
    chunk = 1024
    steps = width // chunk
    extra = kv + 128
    whole = pl.BlockSpec(memory_space=pltpu.VMEM)
    scalars = pl.BlockSpec(memory_space=pltpu.SMEM)
    left = pl.BlockSpec(memory_space=pl.ANY)
    four = [pltpu.VMEM((slots, extra), BF16), pltpu.VMEM((steps, slots, chunk), BF16)] * 4
    dma = pltpu.SemaphoreType.DMA

    slabs = pltpu.VMEM((2, 2, 2, 2, 2, SLAB, 128), F32)

    def chain(route):
        left, bufs = 5, []
        for dim in ("start", *route):
            left -= dim not in LAST and dim != "start"
            lead = (len(LAST[dim]),) if dim in LAST else (2,) * left
            bufs.append(pltpu.VMEM((*lead, THIRD, 128), F32))
        return tuple(bufs)

    return pl.pallas_call(
        main_kernel,
        out_shape=tuple(jax.ShapeDtypeStruct(n.shape, F32) for n in outs),
        in_specs=[scalars] * 3 + [whole, left, whole, left, left, whole],
        out_specs=(whole, whole),
        scratch_shapes=[
            pltpu.VMEM((slots, tokens.shape[0]), BF16),
            pltpu.VMEM(tokens.shape, BF16),
            pltpu.VMEM(at.shape, BF16),
            *four,
            pltpu.VMEM((2, SIDE * SIDE, weight.shape[0], kv // 2), BF16),
            pltpu.VMEM((2, slots, kv // 2), F32),
            pltpu.VMEM((slots, at.shape[0]), F32),
            pltpu.VMEM((at.shape[0], width), F32),
            pltpu.VMEM(b.shape, F32),
            pltpu.VMEM((at.shape[0], 128), F32),
            slabs,
            slabs,
            slabs,
            pltpu.VMEM((width // 128, 8, 128), F32),
            pltpu.VMEM((8, 128), F32),
            pltpu.VMEM((8, 128), F32),
            tuple(chain(r) for r in ROUTES),
            dma((steps + 1,)),
            dma((steps + 1,)),
            dma((steps + 1,)),
            dma((steps + 1,)),
            dma((len(PARTS),)),
            dma((len(PARTS), 16)),
            dma((4,)),
            dma((4, 16)),
            dma((1,)),
            dma((16,)),
            dma((2,)),
            dma((steps + 1,)),
            dma((SUM_SEMS,)),
            dma((SUM_SEMS,)),
        ],
        compiler_params=pltpu.CompilerParams(
            collective_id=0, has_side_effects=True, vmem_limit_bytes=62 << 20
        ),
        name="exchange_and_adapt",
    )(caps, count, bound, user, tokens, goals, weight, at, b)


def body(
    tokens,
    targets,
    row_owner_user,
    device_row_count,
    user_row_cap,
    value_weight,
    adapter_down,
    adapter_up,
    clip_norm_bound,
    down_noise,
    up_noise,
):
    sum_a, sum_b = main(
        user_row_cap, device_row_count, clip_norm_bound, row_owner_user.T, tokens, targets, value_weight,
        adapter_down.T, adapter_up, (down_noise, up_noise.T),
    )
    bound = clip_norm_bound[0]
    return sum_a + bound * down_noise, sum_b.T + bound * up_noise


def solution(mesh):
    in_specs = (
        P(BOTH, None),
        P(BOTH, None),
        P(BOTH, None),
        P(BOTH),
        P(),
        P("fsdp", None),
        P(),
        P(),
        P(),
        P(BOTH, None),
        P(None, BOTH),
    )
    out_specs = (P(BOTH, None), P(None, BOTH))
    return jax.shard_map(
        body, mesh=mesh, in_specs=in_specs, out_specs=out_specs, check_vma=False
    )
```
